256 devices in a mesh: gx: 32 (over z, x), gy: 8 (over y, core).
Axes of the slice: x: 4, y: 4, z: 8, core: 2. Of those that a mesh axis runs over, the one named last changes fastest.
Arguments:
- right_side: float32 [8192, 512], P(('gx', 'gy')), may hold values from -6 to 6
- diagonal: float32 [8192, 512], P(('gx', 'gy')), may hold values from 0.5 to 2
- features: float32 [8192, 64, 512], P(('gx', 'gy')), may hold values from -0.078125 to 0.078125
- neighbours: int32 [8192, 27], P(('gx', 'gy')), may hold values from -1 to 8191, as said below
- vertex_features: float32 [64, 262144], P(None, ('gx', 'gy')), may hold values from -0.75 to 0.75
- vertex_bricks: int32 [262144], P(('gx', 'gy')), may hold values from 0 to 8191, as said below
Outputs:
- solution_field: float32 [8192, 512], P(('gx', 'gy'))
- residual: float32 [8192, 512], P(('gx', 'gy'))
- vertex_values: float32 [262144], P(('gx', 'gy'))
The draws below stay inside these ranges and needn't reach their ends.
Inputs may be any that keep to these rules, and one draw needn't show every extreme that they name: `neighbours`: bricks sit at distinct integer brick coordinates; slot k of a row names the brick at the offset (k // 9 - 1, k // 3 % 3 - 1, k % 3 - 1) from its own, or -1 where no brick is there, so slot 13 names the brick itself and the relation is symmetric. Every brick whose coordinates differ from a brick's by at most two in each direction is held by a device whose gx and gy indices each differ from that brick's holder's by at most one. `vertex_bricks`: vertex n names a brick of its own gx slab: a brick from (n // 8192) * 256 to (n // 8192) * 256 + 255.
All inputs are finite; a program needn't handle non-finite values.
Results may differ from the reference program's by a relative error of at most 0.0002.
Values sent between devices are 32-bit elements; how exact they have to be, the bound alone decides.
No kernel may reach another device: no remote copies, remote signals or barrier semaphores. Data moves between devices by JAX's collectives and lax.ppermute only.
A program may use at most 64 MiB of HBM per device.

```python
import math
import jax
import jax.numpy as jnp
from jax import lax

VOX = 512
FEAT = 64
NBR = 27
ITERS = 3
BDEV = 32
NB = 8192
SLAB = 256
NV = 262144
VSLAB = 8192


def draw_neighbours(key, part):
    devices_all = NB // BDEV
    across = SLAB // BDEV
    along = devices_all // across
    cells = 2 * BDEV
    layers = BDEV // 8
    base = jax.random.fold_in(key, 7)

    def choose(device):
        return jax.random.permutation(jax.random.fold_in(base, device), cells)[:BDEV]
    device_ids = jnp.arange(devices_all, dtype=jnp.int32)
    chosen = jax.vmap(choose)(device_ids).astype(jnp.int32)
    occupancy = jnp.full((devices_all, cells), -1, jnp.int32)
    occupancy = occupancy.at[device_ids[:, None], chosen].set(jnp.arange(BDEV, dtype=jnp.int32)[None, :])
    row_of = (device_ids // across)[:, None]
    col_of = (device_ids % across)[:, None]
    pos_x = row_of * 4 + chosen % 4
    pos_y = col_of * 4 + chosen // 4 % 4
    pos_z = chosen // 16
    slots = jnp.arange(NBR, dtype=jnp.int32)
    step_x = slots // 9 - 1
    step_y = slots // 3 % 3 - 1
    step_z = slots % 3 - 1
    target_x = pos_x[:, :, None] + step_x
    target_y = pos_y[:, :, None] + step_y
    target_z = pos_z[:, :, None] + step_z
    inside = (target_x >= 0) & (target_x < along * 4) & (target_y >= 0) & (target_y < across * 4) & (target_z >= 0) & (target_z < layers)
    safe_x = jnp.clip(target_x, 0, along * 4 - 1)
    safe_y = jnp.clip(target_y, 0, across * 4 - 1)
    safe_z = jnp.clip(target_z, 0, layers - 1)
    target_device = safe_x // 4 * across + safe_y // 4
    target_cell = safe_x % 4 + 4 * (safe_y % 4) + 16 * safe_z
    found = occupancy[target_device, target_cell]
    ids = jnp.where(inside & (found >= 0), target_device * BDEV + found, -1)
    return ids.reshape(NB, NBR).astype(jnp.int32)


def draw_vertex_bricks(key, part):
    vertex_ids = jnp.arange(NV, dtype=jnp.int32)
    within = jax.random.randint(jax.random.fold_in(key, 11), (NV,), 0, SLAB, dtype=jnp.int32)
    return (vertex_ids // VSLAB * SLAB + within).astype(jnp.int32)


def shard_levels(stream_key, shape, split, smallest, high):
    factor_of, own = 1.0, jax.random.fold_in(stream_key, 6)
    for dim, parts in split:
        heights = jnp.exp(jax.random.uniform(jax.random.fold_in(own, dim), (parts,), jnp.float32, smallest / len(split), high / len(split)))
        factor_of = factor_of * jnp.repeat(heights, shape[dim] // parts).reshape([-1 if axis == dim else 1 for axis in range(len(shape))])
    return factor_of


def gaussian(rng, shape, scale, reach, split=(), kind=jnp.bfloat16):
    values = scale * jax.random.normal(rng, shape, jnp.float32)
    if split:
        values = values * shard_levels(rng, shape, split, -0.22, 0.18)
    return jnp.clip(values, -reach, reach).astype(kind)


def setup_inputs(seed: int = 0) -> dict:
    seeds = jax.random.split(jax.random.key(seed), 7)
    return {
        "right_side": gaussian(seeds[0], (NB, VOX), 1.0, 6.0, ((0, 256),), jnp.float32),
        "diagonal": jnp.clip(jnp.exp(math.log(2.0) - 1.3862944 * jax.random.uniform(seeds[1], (NB, VOX), jnp.float32) ** shard_levels(seeds[1], (NB, VOX), ((0, 256),), -0.2, 0.2)), 0.5, 2.0),
        "features": gaussian(seeds[2], (NB, FEAT, VOX), (108 * FEAT) ** -0.5, 0.078125, ((0, 256),), jnp.float32),
        "neighbours": draw_neighbours(jax.random.fold_in(seeds[6], 71), 0),
        "vertex_features": gaussian(seeds[4], (FEAT, NV), FEAT ** -0.5, 0.75, ((1, 256),), jnp.float32),
        "vertex_bricks": draw_vertex_bricks(jax.random.fold_in(seeds[6], 71), 0),
    }


def neighbour_sum(values, neighbours):
    valid = neighbours >= 0
    picked = jnp.take(values, jnp.where(valid, neighbours, 0).astype(jnp.int32), axis=0)
    return jnp.sum(jnp.where(valid[:, :, None], picked, jnp.zeros_like(picked)), axis=1)


def coefficient(features, field):
    return jnp.einsum("bfv,bv->bf", features, field, precision=lax.Precision.HIGHEST)


def operate(field, diagonal, features, neighbours):
    first = neighbour_sum(coefficient(features, field), neighbours)
    second = neighbour_sum(first, neighbours)
    return diagonal * field + jnp.einsum("bfv,bf->bv", features, second, precision=lax.Precision.HIGHEST)


def reference(right_side, diagonal, features, neighbours, vertex_features, vertex_bricks):
    solution_field = jnp.zeros_like(right_side)
    residual, direction = right_side, right_side
    norm_now = jnp.sum(residual * residual)
    for step in range(ITERS):
        image = operate(direction, diagonal, features, neighbours)
        alpha = norm_now / jnp.sum(direction * image)
        solution_field = solution_field + alpha * direction
        residual = residual - alpha * image
        norm_next = jnp.sum(residual * residual)
        direction = residual + (norm_next / norm_now) * direction
        norm_now = norm_next
    surface = neighbour_sum(coefficient(features, solution_field), neighbours)
    picked = jnp.take(surface, vertex_bricks.astype(jnp.int32), axis=0)
    vertex_values = jnp.sum(vertex_features * picked.T, axis=0)
    return solution_field, residual, vertex_values
```

```python
import jax
import jax.numpy as jnp
from jax import lax
from jax.sharding import PartitionSpec as P

ITERS = 3
SHIFT = 1.25
HIGHEST = lax.Precision.HIGHEST


def ring(axis, step):
    count = lax.axis_size(axis)
    return [(i, (i + step) % count) for i in range(count)]


def with_halo(block):
    column = jnp.stack(
        [lax.ppermute(block, "gx", ring("gx", 1)), block, lax.ppermute(block, "gx", ring("gx", -1))]
    )
    square = jnp.stack(
        [lax.ppermute(column, "gy", ring("gy", 1)), column, lax.ppermute(column, "gy", ring("gy", -1))],
        axis=1,
    )
    return square.reshape(9 * block.shape[0], block.shape[1])


def spread(values, axis):
    count = lax.axis_size(axis)
    return lax.all_to_all(jnp.broadcast_to(values[None], (count,) + values.shape), axis, 0, 0)


def coefficient(features, field):
    return jnp.einsum("bfv,bv->bf", features, field, precision=HIGHEST)


def expand(features, coeff):
    return jnp.einsum("bfv,bf->bv", features, coeff, precision=HIGHEST)


def one_hot_counts(ids, nrows):
    across = lax.axis_size("gy")
    owner = ids // nrows
    offset_x = owner // across - lax.axis_index("gx") + 1
    offset_y = owner % across - lax.axis_index("gy") + 1
    inside = (ids >= 0) & (offset_x >= 0) & (offset_x < 3) & (offset_y >= 0) & (offset_y < 3)
    position = jnp.where(inside, (offset_x * 3 + offset_y) * nrows + ids % nrows, -1)
    targets = jnp.arange(9 * nrows, dtype=jnp.int32)
    hits = position[:, :, None] == targets[None, None, :]
    return jnp.sum(hits.astype(jnp.float32), axis=1)


def cg_weights(mu):
    def dot(left, right):
        return sum(left[i] * right[j] * mu[i + j] for i in range(len(left)) for j in range(len(right)))

    def apply(poly):
        out = [SHIFT * p for p in poly] + [0.0]
        for i, p in enumerate(poly):
            out[i + 1] = out[i + 1] + p
        return out

    def axpy(left, scale, right):
        size = max(len(left), len(right))
        left = left + [0.0] * (size - len(left))
        return [l + scale * right[i] if i < len(right) else l for i, l in enumerate(left)]

    field, residual, direction, norm_now = [], [1.0], [1.0], mu[0]
    for step in range(ITERS):
        image = apply(direction)
        alpha = norm_now / dot(direction, image)
        field = axpy(field, alpha, direction)
        residual = axpy(residual, -alpha, image)
        if step + 1 < ITERS:
            norm_next = dot(residual, residual)
            direction = axpy(residual, norm_next / norm_now, direction)
            norm_now = norm_next
    return field, residual


def per_device(right_side, diagonal, features, neighbours, vertex_features, vertex_bricks):
    nrows, width, _ = features.shape
    slots = neighbours.shape[1]
    shifted = diagonal - SHIFT
    powers = [right_side]
    sums = []
    moments = [jnp.sum(right_side * right_side)]
    own = one_hot_counts(neighbours, nrows)
    for step in range(ITERS):
        coeff = coefficient(features, powers[-1])
        extra = neighbours.astype(jnp.float32) if step == 0 else jnp.zeros((nrows, slots), jnp.float32)
        block = jnp.concatenate([coeff, jnp.pad(extra, ((0, 0), (0, 128 - width - slots)))], axis=1)
        around = with_halo(block)
        if step == 0:
            near = one_hot_counts(around[:, width : width + slots].astype(jnp.int32), nrows)
            twice = jnp.dot(own, near, precision=HIGHEST)
        sums.append(jnp.dot(own, around[:, :width], precision=HIGHEST))
        second = jnp.dot(twice, around[:, :width], precision=HIGHEST)
        new = shifted * powers[-1] + expand(features, second)
        moments.append(jnp.sum(powers[-1] * new))
        if step + 1 < ITERS:
            moments.append(jnp.sum(new * new))
        powers.append(new)
    part = jnp.pad(jnp.stack(moments), (0, 128 - len(moments)))
    packed = jnp.concatenate(sums, axis=1).reshape(-1, 128)
    packed = jnp.concatenate([packed, jnp.broadcast_to(part[None], (8, 128))], axis=0)
    slab = spread(packed, "gy")
    part = jnp.sum(slab[:, -1, :], axis=0, keepdims=True)
    total = jnp.sum(spread(part, "gx")[:, 0, :], axis=0)
    field, residual = cg_weights([total[i] for i in range(len(moments))])
    solution_field = sum(w * v for w, v in zip(field, powers))
    residual = sum(w * v for w, v in zip(residual, powers))
    slab_sums = slab[:, :-8, :].reshape(-1, ITERS * width)
    surface = sum(w * slab_sums[:, i * width : (i + 1) * width] for i, w in enumerate(field))
    local_ids = vertex_bricks - lax.axis_index("gx") * surface.shape[0]
    picks = (jnp.arange(surface.shape[0], dtype=jnp.int32)[:, None] == local_ids[None, :]).astype(jnp.float32)
    picked = lax.dot_general(surface, picks, (((0,), (0,)), ((), ())), precision=HIGHEST)
    vertex_values = jnp.sum(vertex_features * picked, axis=0)
    return solution_field, residual, vertex_values


def solution(mesh):
    placed = (
        P(("gx", "gy"), None),
        P(("gx", "gy"), None),
        P(("gx", "gy"), None, None),
        P(("gx", "gy"), None),
        P(None, ("gx", "gy")),
        P(("gx", "gy")),
    )
    return jax.shard_map(
        per_device,
        mesh=mesh,
        in_specs=placed,
        out_specs=(P(("gx", "gy"), None), P(("gx", "gy"), None), P(("gx", "gy"))),
        check_vma=False,
    )
```

```python
import functools

import jax
import jax.numpy as jnp
from jax import lax
from jax.experimental import pallas as pl
from jax.experimental.pallas import tpu as pltpu
from jax.sharding import PartitionSpec as P

ITERS = 3
SHIFT = 1.25
LANES = 128
MOMENTS = 2 * ITERS
CHUNKS = 8
VMEM = pl.BlockSpec(memory_space=pltpu.VMEM)
PARAMS = pltpu.CompilerParams(vmem_limit_bytes=24 * 1024 * 1024)
F32, BF16 = jnp.float32, jnp.bfloat16


def call(kernel, out_shape, *args, specs=None, scratch=()):
    many = isinstance(out_shape, (list, tuple))
    return pl.pallas_call(
        kernel,
        out_shape=out_shape,
        in_specs=specs or [VMEM] * len(args),
        out_specs=[VMEM] * len(out_shape) if many else VMEM,
        scratch_shapes=scratch,
        compiler_params=PARAMS,
    )(*args)


def f32(*shape):
    return jax.ShapeDtypeStruct(shape, F32)


def ring(axis, step):
    count = lax.axis_size(axis)
    return [(i, (i + step) % count) for i in range(count)]


def lane_iota(rows, lanes=LANES):
    return lax.broadcasted_iota(jnp.int32, (rows, lanes), 1)


def total(values):
    folded = values[:, :LANES]
    for start in range(LANES, values.shape[1], LANES):
        folded = folded + values[:, start : start + LANES]
    return jnp.sum(jnp.sum(folded, axis=0, keepdims=True), axis=1, keepdims=True)


def put(row, lane, value):
    return jnp.where(lane_iota(1) == lane, value, row)


def project(feature, field, columns, brick):
    product = feature * field
    folded = product[:, :LANES]
    for start in range(LANES, product.shape[1], LANES):
        folded = folded + product[:, start : start + LANES]
    column = jnp.sum(folded, axis=1, keepdims=True)
    return jnp.where(lane_iota(columns.shape[0]) == brick, column, columns)


def to_rows(columns, nrows):
    square = jnp.concatenate([columns, jnp.zeros((LANES - columns.shape[0], LANES), F32)], axis=0)
    return square.T[:nrows]


def first_kernel(features, field, neighbours, block, moments, buffer, sems):
    nrows, width, _ = features.shape
    each = nrows // CHUNKS
    copies = [
        pltpu.make_async_copy(
            features.at[pl.ds(i * each, each)], buffer.at[pl.ds(i * each, each)], sems.at[i]
        )
        for i in range(CHUNKS)
    ]
    for copy in copies:
        copy.start()
    value = field[...]
    moments[...] = put(jnp.zeros((1, LANES), F32), 0, total(value * value))
    columns = jnp.zeros((width, LANES), F32)
    for i, copy in enumerate(copies):
        copy.wait()
        for b in range(i * each, (i + 1) * each):
            columns = project(buffer[b], field[b : b + 1, :], columns, b)
    block[...] = to_rows(columns, nrows)
    block[:, width : width + neighbours.shape[1]] = neighbours[...].astype(F32)


def one_hot(block, nrows, width, slots, span, across, row_index, col_index):
    ids = block.astype(jnp.int32)
    bits = nrows.bit_length() - 1
    owner = lax.shift_right_arithmetic(ids, bits)
    offset_x = lax.shift_right_arithmetic(owner, across.bit_length() - 1) - row_index + 1
    offset_y = (owner & (across - 1)) - col_index + 1
    inside = (ids >= 0) & (offset_x >= 0) & (offset_x < 3) & (offset_y >= 0) & (offset_y < 3)
    position = jnp.where(inside, (offset_y * 3 + offset_x) * nrows + (ids & (nrows - 1)), -1)
    lanes = lane_iota(block.shape[0], span)
    out = jnp.zeros((block.shape[0], span), F32)
    for slot in range(width, width + slots):
        out = jnp.where(position[:, slot : slot + 1] == lanes, 1.0, out)
    return out.astype(BF16)


def middle_kernel(hot, index, column, out):
    out[...] = hot(column[...], row_index=index[0], col_index=index[1])


def advance(step, nrows, width, weights, around, features, diagonal, before, sums, moments, outs):
    last = step + 1 == ITERS
    parts = []
    rest = around
    for _ in range(3):
        part = rest.astype(BF16)
        rest = rest - part.astype(F32)
        parts.append(part)
    result = jnp.dot(weights, parts[0], preferred_element_type=F32)
    for part in parts[1:]:
        result = result + jnp.dot(weights, part, preferred_element_type=F32)
    turned = result.T[:width]
    lanes = lane_iota(width)
    shift = step * nrows
    moved = pltpu.roll(turned, shift, 1) if shift else turned
    sums = jnp.where((lanes >= shift) & (lanes < shift + nrows), moved, sums)
    old = before[...]
    base = (diagonal[...] - SHIFT) * old
    columns = jnp.zeros((width, LANES), F32)
    for b in range(nrows):
        second = turned[:, nrows + b : nrows + b + 1]
        image = jnp.sum(features[b] * second, axis=0, keepdims=True)
        new = base[b : b + 1, :] + image
        outs[0][b : b + 1, :] = new
        if not last:
            columns = project(features[b], new, columns, b)
    new = outs[0][...]
    moments = put(moments, 2 * step + 1, total(old * new))
    if not last:
        moments = put(moments, 2 * step + 2, total(new * new))
    return sums, moments, columns


def second_kernel(
    hot, index, left, column, right, middle, features, diagonal, before, moments,
    new, block, sums_out, moments_out, weights_out,
):
    nrows, width, _ = features.shape
    rows, cols = index[0], index[1]
    own = middle[nrows : 2 * nrows, :]
    near = [
        hot(left[...], row_index=rows, col_index=cols),
        middle[...],
        hot(right[...], row_index=rows, col_index=cols),
    ]
    near = jnp.concatenate(near, axis=0)
    twice = jnp.dot(own, near, preferred_element_type=F32).astype(BF16)
    pad = jnp.zeros((LANES - 2 * nrows, near.shape[1]), BF16)
    weights = jnp.concatenate([own, twice, pad], axis=0)
    weights_out[...] = weights
    around = jnp.concatenate([left[...], column[...], right[...]], axis=0)
    sums, moment, columns = advance(
        0, nrows, width, weights, around, features, diagonal, before,
        jnp.zeros((width, LANES), F32), moments[...], [new],
    )
    block[...] = to_rows(columns, nrows)
    sums_out[...] = sums
    moments_out[...] = moment


def third_kernel(
    left, column, right, weights, features, diagonal, before, sums, moments,
    new, block, sums_out, moments_out,
):
    nrows, width, _ = features.shape
    around = jnp.concatenate([left[...], column[...], right[...]], axis=0)
    total_sums, moment, columns = advance(
        1, nrows, width, weights[...], around, features, diagonal, before,
        sums[...], moments[...], [new],
    )
    block[...] = to_rows(columns, nrows)
    sums_out[...] = total_sums
    moments_out[...] = moment


def fourth_kernel(
    left, column, right, weights, features, diagonal, before, sums, moments,
    new, sums_out, moments_out,
):
    nrows, width, _ = features.shape
    around = jnp.concatenate([left[...], column[...], right[...]], axis=0)
    total_sums, moment, _ = advance(
        2, nrows, width, weights[...], around, features, diagonal, before,
        sums[...], moments[...], [new],
    )
    sums_out[...] = jnp.broadcast_to(total_sums[None], sums_out.shape)
    moments_out[...] = jnp.broadcast_to(moment, moments_out.shape)


def vertex_kernel(nrows, index, slab, bricks, vertex_features, out):
    across, width, _ = slab.shape
    local = bricks[...] - index[0] * across * nrows
    hot = lax.broadcasted_iota(jnp.int32, (across * nrows, local.shape[1]), 0) == local
    hot = jnp.where(hot, 1.0, 0.0).astype(BF16)
    group = LANES // nrows
    lanes = lane_iota(width)
    table = []
    for k in range(ITERS):
        tiles = []
        for start in range(0, across, group):
            tile = jnp.zeros((width, LANES), F32)
            for d in range(group):
                shift = (d - k) * nrows % LANES
                moved = pltpu.roll(slab[start + d], shift, 1) if shift else slab[start + d]
                tile = jnp.where((lanes >= d * nrows) & (lanes < (d + 1) * nrows), moved, tile)
            tiles.append(tile)
        table.append(jnp.concatenate(tiles, axis=1))
    rest = jnp.concatenate(table, axis=0)
    picked = None
    for _ in range(3):
        part = rest.astype(BF16)
        rest = rest - part.astype(F32)
        value = jnp.dot(part, hot, preferred_element_type=F32)
        picked = value if picked is None else picked + value
    for k in range(ITERS):
        product = vertex_features[...] * picked[k * width : (k + 1) * width, :]
        out[k : k + 1, :] = jnp.sum(product, axis=0, keepdims=True)


def cg_weights(mu):
    def dot(left, right):
        return sum(left[i] * right[j] * mu[i + j] for i in range(len(left)) for j in range(len(right)))

    def apply(poly):
        out = [SHIFT * p for p in poly] + [0.0]
        for i, p in enumerate(poly):
            out[i + 1] = out[i + 1] + p
        return out

    def axpy(left, scale, right):
        size = max(len(left), len(right))
        left = left + [0.0] * (size - len(left))
        return [l + scale * right[i] if i < len(right) else l for i, l in enumerate(left)]

    field, residual, direction, norm_now = [], [1.0], [1.0], mu[0]
    for step in range(ITERS):
        image = apply(direction)
        alpha = norm_now / dot(direction, image)
        field = axpy(field, alpha, direction)
        residual = axpy(residual, -alpha, image)
        if step + 1 < ITERS:
            norm_next = dot(residual, residual)
            direction = axpy(residual, norm_next / norm_now, direction)
            norm_now = norm_next
    return field, residual


def last_kernel(moments, v0, v1, v2, v3, vertices, field_out, residual_out, vertices_out):
    sums = jnp.sum(moments[...], axis=0, keepdims=True)
    field, residual = cg_weights([sums[:, i : i + 1] for i in range(MOMENTS)])
    powers = [v0[...], v1[...], v2[...], v3[...]]
    field_out[...] = sum(w * v for w, v in zip(field, powers))
    residual_out[...] = sum(w * v for w, v in zip(residual, powers))
    vertices_out[...] = sum(w * vertices[i : i + 1, :] for i, w in enumerate(field))


def neighbourhood(block):
    column = jnp.concatenate(
        [lax.ppermute(block, "gx", ring("gx", 1)), block, lax.ppermute(block, "gx", ring("gx", -1))]
    )
    return (
        lax.ppermute(column, "gy", ring("gy", 1)),
        column,
        lax.ppermute(column, "gy", ring("gy", -1)),
    )


def per_device(right_side, diagonal, features, neighbours, vertex_features, vertex_bricks):
    nrows, width, voxels = features.shape
    slots = neighbours.shape[1]
    across = lax.axis_size("gy")
    devices = across * lax.axis_size("gx")
    index = jnp.stack([lax.axis_index("gx"), lax.axis_index("gy")]).astype(jnp.int32)
    smem = pl.BlockSpec(memory_space=pltpu.SMEM)
    hot = functools.partial(
        one_hot, nrows=nrows, width=width, slots=slots, span=9 * nrows, across=across
    )
    power = f32(nrows, voxels)
    block_shape, row, table = f32(nrows, LANES), f32(1, LANES), f32(width, LANES)

    block, moments = call(
        first_kernel, [block_shape, row], features, right_side, neighbours,
        specs=[pl.BlockSpec(memory_space=pl.ANY), VMEM, VMEM],
        scratch=[pltpu.VMEM(features.shape, F32), pltpu.SemaphoreType.DMA((CHUNKS,))],
    )
    left, column, right = neighbourhood(block)
    middle = call(
        functools.partial(middle_kernel, hot),
        jax.ShapeDtypeStruct((3 * nrows, 9 * nrows), BF16), index, column, specs=[smem, VMEM],
    )
    v1, block, sums, moments, weights = call(
        functools.partial(second_kernel, hot),
        [power, block_shape, table, row, jax.ShapeDtypeStruct((LANES, 9 * nrows), BF16)],
        index, left, column, right, middle, features, diagonal, right_side, moments,
        specs=[smem] + [VMEM] * 8,
    )
    left, column, right = neighbourhood(block)
    v2, block, sums, moments = call(
        third_kernel, [power, block_shape, table, row],
        left, column, right, weights, features, diagonal, v1, sums, moments,
    )
    left, column, right = neighbourhood(block)
    v3, sums, moments = call(
        fourth_kernel, [power, f32(across, width, LANES), f32(devices, LANES)],
        left, column, right, weights, features, diagonal, v2, sums, moments,
    )
    moments = lax.all_to_all(moments, ("gx", "gy"), 0, 0, tiled=True)
    slab = lax.all_to_all(sums, "gy", 0, 0, tiled=True)
    vertices = call(
        functools.partial(vertex_kernel, nrows), f32(8, vertex_bricks.shape[0]),
        index, slab, vertex_bricks.reshape(1, -1), vertex_features, specs=[smem] + [VMEM] * 3,
    )
    field, residual, values = call(
        last_kernel, [power, power, f32(1, vertex_bricks.shape[0])],
        moments, right_side, v1, v2, v3, vertices,
    )
    return field, residual, values.reshape(-1)


def solution(mesh):
    placed = (
        P(("gx", "gy"), None),
        P(("gx", "gy"), None),
        P(("gx", "gy"), None, None),
        P(("gx", "gy"), None),
        P(None, ("gx", "gy")),
        P(("gx", "gy")),
    )
    return jax.shard_map(
        per_device,
        mesh=mesh,
        in_specs=placed,
        out_specs=(P(("gx", "gy"), None), P(("gx", "gy"), None), P(("gx", "gy"))),
        check_vma=False,
    )
```

```python
import functools

import jax
import jax.numpy as jnp
from jax import lax
from jax.experimental import pallas as pl
from jax.experimental.pallas import tpu as pltpu
from jax.sharding import PartitionSpec as P

ITERS = 3
SHIFT = 1.25
LANES = 128
MOMENTS = 2 * ITERS
CHUNKS = 8
MOMENT_LANE = 96
FIRST_LIMIT = 60
VMEM = pl.BlockSpec(memory_space=pltpu.VMEM)
F32, BF16 = jnp.float32, jnp.bfloat16


def call(kernel, out_shape, *args, specs=None, scratch=(), limit=24):
    many = isinstance(out_shape, (list, tuple))
    return pl.pallas_call(
        kernel,
        out_shape=out_shape,
        in_specs=specs or [VMEM] * len(args),
        out_specs=[VMEM] * len(out_shape) if many else VMEM,
        scratch_shapes=scratch,
        compiler_params=pltpu.CompilerParams(vmem_limit_bytes=limit * 1024 * 1024),
    )(*args)


def f32(*shape):
    return jax.ShapeDtypeStruct(shape, F32)


def ring(axis, step):
    count = lax.axis_size(axis)
    return [(i, (i + step) % count) for i in range(count)]


def lane_iota(rows, lanes=LANES):
    return lax.broadcasted_iota(jnp.int32, (rows, lanes), 1)


def total(values):
    folded = values[:, :LANES]
    for start in range(LANES, values.shape[1], LANES):
        folded = folded + values[:, start : start + LANES]
    return jnp.sum(jnp.sum(folded, axis=0, keepdims=True), axis=1, keepdims=True)


def put(row, lane, value):
    return jnp.where(lane_iota(1) == lane, value, row)


def project(feature, field, columns, brick):
    product = feature * field
    folded = product[:, :LANES]
    for start in range(LANES, product.shape[1], LANES):
        folded = folded + product[:, start : start + LANES]
    column = jnp.sum(folded, axis=1, keepdims=True)
    return jnp.where(lane_iota(columns.shape[0]) == brick, column, columns)


def to_rows(columns, nrows):
    square = jnp.concatenate([columns, jnp.zeros((LANES - columns.shape[0], LANES), F32)], axis=0)
    return square.T[:nrows]


def first_kernel(features, field, neighbours, block, moments, values, ids, buffer, sems):
    nrows, width, _ = features.shape
    each = nrows // CHUNKS
    copies = [
        pltpu.make_async_copy(
            features.at[pl.ds(i * each, each)], buffer.at[pl.ds(i * each, each)], sems.at[i]
        )
        for i in range(CHUNKS)
    ]
    small = [
        pltpu.make_async_copy(field, values, sems.at[CHUNKS]),
        pltpu.make_async_copy(neighbours, ids, sems.at[CHUNKS + 1]),
    ]
    for copy in small + copies:
        copy.start()
    for copy in small:
        copy.wait()
    value = values[...]
    moments[...] = put(jnp.zeros((1, LANES), F32), MOMENT_LANE, total(value * value))
    columns = jnp.zeros((width, LANES), F32)
    for i, copy in enumerate(copies):
        copy.wait()
        for b in range(i * each, (i + 1) * each):
            columns = project(buffer[b], values[b : b + 1, :], columns, b)
    block[...] = to_rows(columns, nrows)
    block[:, width : width + neighbours.shape[1]] = ids[...].astype(F32)


def positions(block, nrows, across, row_index, col_index):
    ids = block.astype(jnp.int32)
    owner = lax.shift_right_arithmetic(ids, nrows.bit_length() - 1)
    offset_x = lax.shift_right_arithmetic(owner, across.bit_length() - 1) - row_index + 1
    offset_y = (owner & (across - 1)) - col_index + 1
    inside = (ids >= 0) & (offset_x >= 0) & (offset_x < 3) & (offset_y >= 0) & (offset_y < 3)
    return jnp.where(inside, offset_y * LANES + offset_x * nrows + (ids & (nrows - 1)), -1)


def one_hot(position, first, lanes, width, slots):
    targets = lane_iota(position.shape[0], lanes) + first
    out = jnp.zeros((position.shape[0], lanes), F32)
    for slot in range(width, width + slots):
        out = jnp.where(position[:, slot : slot + 1] == targets, 1.0, out)
    return out.astype(BF16)


def padded(third):
    return jnp.concatenate([third, jnp.zeros((LANES - third.shape[0], third.shape[1]), third.dtype)])


def own_kernel(shape, index, block, features, out):
    nrows, width, slots, across = shape
    place = positions(block[...], nrows, across, index[0], index[1])
    out[...] = one_hot(place, 0, 3 * LANES, width, slots)


def middle_kernel(shape, index, column, own, out):
    nrows, width, slots, across = shape
    others = jnp.concatenate([column[:nrows, :], column[2 * nrows :, :]], axis=0)
    place = positions(others, nrows, across, index[0], index[1])
    hot = one_hot(place, 0, 3 * LANES, width, slots)
    out[...] = padded(jnp.concatenate([hot[:nrows], own[...], hot[nrows:]], axis=0))


def advance(step, nrows, width, weights, around, features, diagonal, before, sums, moments, outs):
    last = step + 1 == ITERS
    parts = []
    rest = around
    for _ in range(3):
        part = rest.astype(BF16)
        rest = rest - part.astype(F32)
        parts.append(part)
    result = jnp.dot(weights, parts[0], preferred_element_type=F32)
    for part in parts[1:]:
        result = result + jnp.dot(weights, part, preferred_element_type=F32)
    turned = result.T[:width]
    lanes = lane_iota(width)
    shift = step * nrows
    moved = pltpu.roll(turned, shift, 1) if shift else turned
    sums = jnp.where((lanes >= shift) & (lanes < shift + nrows), moved, sums)
    old = before[...]
    base = (diagonal[...] - SHIFT) * old
    columns = jnp.zeros((width, LANES), F32)
    for b in range(nrows):
        second = turned[:, nrows + b : nrows + b + 1]
        image = jnp.sum(features[b] * second, axis=0, keepdims=True)
        new = base[b : b + 1, :] + image
        outs[0][b : b + 1, :] = new
        if not last:
            columns = project(features[b], new, columns, b)
    new = outs[0][...]
    moments = put(moments, MOMENT_LANE + 2 * step + 1, total(old * new))
    if not last:
        moments = put(moments, MOMENT_LANE + 2 * step + 2, total(new * new))
    return sums, moments, columns


def second_kernel(
    shape, index, left, column, right, middle, features, diagonal, before, moments,
    new, block, sums_out, moments_out, weights_out,
):
    nrows, width, slots, across = shape
    own = middle[nrows : 2 * nrows, :]
    pieces = [own[:, d * LANES : (d + 1) * LANES] for d in range(3)]
    centre = middle[...]
    thirds = [jnp.dot(pieces[1], centre[:, d * LANES : (d + 1) * LANES], preferred_element_type=F32) for d in range(3)]
    for d, side in ((0, left), (2, right)):
        place = positions(side[...], nrows, across, index[0], index[1])
        hot = padded(one_hot(place, d * LANES, LANES, width, slots))
        thirds[d] = thirds[d] + jnp.dot(pieces[d], hot, preferred_element_type=F32)
        across_dy = centre[:, d * LANES : (d + 1) * LANES]
        thirds[1] = thirds[1] + lax.dot_general(
            pieces[d], across_dy, (((1,), (1,)), ((), ())), preferred_element_type=F32
        )
    twice = jnp.concatenate(thirds, axis=1).astype(BF16)
    pad = jnp.zeros((LANES - 2 * nrows, 3 * LANES), BF16)
    weights = jnp.concatenate([own, twice, pad], axis=0)
    weights_out[...] = weights
    around = jnp.concatenate([padded(side[...]) for side in (left, column, right)], axis=0)
    sums, moment, columns = advance(
        0, nrows, width, weights, around, features, diagonal, before,
        jnp.zeros((width, LANES), F32), moments[...], [new],
    )
    block[...] = to_rows(columns, nrows)
    sums_out[...] = sums
    moments_out[...] = moment


def third_kernel(
    left, column, right, weights, features, diagonal, before, sums, moments,
    new, block, sums_out, moments_out,
):
    nrows, width, _ = features.shape
    around = jnp.concatenate([padded(side[...]) for side in (left, column, right)], axis=0)
    total_sums, moment, columns = advance(
        1, nrows, width, weights[...], around, features, diagonal, before,
        sums[...], moments[...], [new],
    )
    block[...] = to_rows(columns, nrows)
    sums_out[...] = total_sums
    moments_out[...] = moment


def fourth_kernel(
    left, column, right, weights, features, diagonal, before, sums, moments,
    new, sums_out,
):
    nrows, width, _ = features.shape
    around = jnp.concatenate([padded(side[...]) for side in (left, column, right)], axis=0)
    total_sums, moment, _ = advance(
        2, nrows, width, weights[...], around, features, diagonal, before,
        sums[...], moments[...], [new],
    )
    rows = lax.broadcasted_iota(jnp.int32, total_sums.shape, 0)
    mixed = total_sums + jnp.where(rows == 0, moment, 0.0)
    sums_out[...] = jnp.broadcast_to(mixed[None], sums_out.shape)


def fold_kernel(slab, out):
    row = slab[0, 0:1, :]
    for d in range(1, slab.shape[0]):
        row = row + slab[d, 0:1, :]
    out[...] = jnp.broadcast_to(row, out.shape)


def vertex_kernel(nrows, index, slab, bricks, vertex_features, out):
    across, width, _ = slab.shape
    local = bricks[...] - index[0] * across * nrows
    hot = lax.broadcasted_iota(jnp.int32, (across * nrows, local.shape[1]), 0) == local
    hot = jnp.where(hot, 1.0, 0.0).astype(BF16)
    group = LANES // nrows
    lanes = lane_iota(width)
    table = []
    for k in range(ITERS):
        tiles = []
        for start in range(0, across, group):
            tile = jnp.zeros((width, LANES), F32)
            for d in range(group):
                shift = (d - k) * nrows % LANES
                moved = pltpu.roll(slab[start + d], shift, 1) if shift else slab[start + d]
                tile = jnp.where((lanes >= d * nrows) & (lanes < (d + 1) * nrows), moved, tile)
            tiles.append(tile)
        table.append(jnp.concatenate(tiles, axis=1))
    rest = jnp.concatenate(table, axis=0)
    picked = None
    for _ in range(3):
        part = rest.astype(BF16)
        rest = rest - part.astype(F32)
        value = jnp.dot(part, hot, preferred_element_type=F32)
        picked = value if picked is None else picked + value
    for k in range(ITERS):
        product = vertex_features[...] * picked[k * width : (k + 1) * width, :]
        out[k : k + 1, :] = jnp.sum(product, axis=0, keepdims=True)


def cg_weights(mu):
    def dot(left, right):
        return sum(left[i] * right[j] * mu[i + j] for i in range(len(left)) for j in range(len(right)))

    def apply(poly):
        out = [SHIFT * p for p in poly] + [0.0]
        for i, p in enumerate(poly):
            out[i + 1] = out[i + 1] + p
        return out

    def axpy(left, scale, right):
        size = max(len(left), len(right))
        left = left + [0.0] * (size - len(left))
        return [l + scale * right[i] if i < len(right) else l for i, l in enumerate(left)]

    field, residual, direction, norm_now = [], [1.0], [1.0], mu[0]
    for step in range(ITERS):
        image = apply(direction)
        alpha = norm_now / dot(direction, image)
        field = axpy(field, alpha, direction)
        residual = axpy(residual, -alpha, image)
        if step + 1 < ITERS:
            norm_next = dot(residual, residual)
            direction = axpy(residual, norm_next / norm_now, direction)
            norm_now = norm_next
    return field, residual


def last_kernel(moments, v0, v1, v2, v3, vertices, field_out, residual_out, vertices_out):
    sums = jnp.sum(moments[...], axis=0, keepdims=True)
    field, residual = cg_weights([sums[:, MOMENT_LANE + i : MOMENT_LANE + i + 1] for i in range(MOMENTS)])
    powers = [v0[...], v1[...], v2[...], v3[...]]
    field_out[...] = sum(w * v for w, v in zip(field, powers))
    residual_out[...] = sum(w * v for w, v in zip(residual, powers))
    vertices_out[...] = sum(w * vertices[i : i + 1, :] for i, w in enumerate(field))


def neighbourhood(block):
    column = jnp.concatenate(
        [lax.ppermute(block, "gx", ring("gx", 1)), block, lax.ppermute(block, "gx", ring("gx", -1))]
    )
    return (
        lax.ppermute(column, "gy", ring("gy", 1)),
        column,
        lax.ppermute(column, "gy", ring("gy", -1)),
    )


def per_device(right_side, diagonal, features, neighbours, vertex_features, vertex_bricks):
    nrows, width, voxels = features.shape
    slots = neighbours.shape[1]
    across, along = lax.axis_size("gy"), lax.axis_size("gx")
    index = jnp.stack([lax.axis_index("gx"), lax.axis_index("gy")]).astype(jnp.int32)
    smem, hbm = pl.BlockSpec(memory_space=pltpu.SMEM), pl.BlockSpec(memory_space=pltpu.HBM)
    shape = (nrows, width, slots, across)
    power = f32(nrows, voxels)
    block_shape, row, table = f32(nrows, LANES), f32(1, LANES), f32(width, LANES)

    block, moments = call(
        first_kernel, [block_shape, row], features, right_side, neighbours,
        specs=[hbm] * 3, limit=FIRST_LIMIT,
        scratch=[
            pltpu.VMEM(right_side.shape, F32),
            pltpu.VMEM(neighbours.shape, jnp.int32),
            pltpu.VMEM(features.shape, F32),
            pltpu.SemaphoreType.DMA((CHUNKS + 2,)),
        ],
    )
    own = call(
        functools.partial(own_kernel, shape), jax.ShapeDtypeStruct((nrows, 3 * LANES), BF16),
        index, block, features, specs=[smem, VMEM, VMEM],
    )
    left, column, right = neighbourhood(block)
    middle = call(
        functools.partial(middle_kernel, shape), jax.ShapeDtypeStruct((LANES, 3 * LANES), BF16),
        index, column, own, specs=[smem, VMEM, VMEM],
    )
    v1, block, sums, moments, weights = call(
        functools.partial(second_kernel, shape),
        [power, block_shape, table, row, jax.ShapeDtypeStruct((LANES, 3 * LANES), BF16)],
        index, left, column, right, middle, features, diagonal, right_side, moments,
        specs=[smem] + [VMEM] * 8,
    )
    left, column, right = neighbourhood(block)
    v2, block, sums, moments = call(
        third_kernel, [power, block_shape, table, row],
        left, column, right, weights, features, diagonal, v1, sums, moments,
    )
    left, column, right = neighbourhood(block)
    v3, sums = call(
        fourth_kernel, [power, f32(across, width, LANES)],
        left, column, right, weights, features, diagonal, v2, sums, moments,
    )
    slab = lax.all_to_all(sums, "gy", 0, 0, tiled=True)
    moments = lax.all_to_all(call(fold_kernel, f32(along, LANES), slab), "gx", 0, 0, tiled=True)
    vertices = call(
        functools.partial(vertex_kernel, nrows), f32(8, vertex_bricks.shape[0]),
        index, slab, vertex_bricks.reshape(1, -1), vertex_features, specs=[smem] + [VMEM] * 3,
    )
    field, residual, values = call(
        last_kernel, [power, power, f32(1, vertex_bricks.shape[0])],
        moments, right_side, v1, v2, v3, vertices,
    )
    return field, residual, values.reshape(-1)


def solution(mesh):
    placed = (
        P(("gx", "gy"), None),
        P(("gx", "gy"), None),
        P(("gx", "gy"), None, None),
        P(("gx", "gy"), None),
        P(None, ("gx", "gy")),
        P(("gx", "gy")),
    )
    return jax.shard_map(
        per_device,
        mesh=mesh,
        in_specs=placed,
        out_specs=(P(("gx", "gy"), None), P(("gx", "gy"), None), P(("gx", "gy"))),
        check_vma=False,
    )
```

```python
import functools

import jax
import jax.numpy as jnp
from jax import lax
from jax.experimental import pallas as pl
from jax.experimental.pallas import tpu as pltpu
from jax.sharding import PartitionSpec as P

ITERS = 3
SHIFT = 1.25
LANES = 128
MOMENTS = 2 * ITERS
CHUNKS = 8
AHEAD = 3
MOMENT_LANE = 96
FIRST_LIMIT = 60
VMEM = pl.BlockSpec(memory_space=pltpu.VMEM)
F32, BF16 = jnp.float32, jnp.bfloat16


def call(kernel, out_shape, *args, specs=None, scratch=(), limit=24):
    many = isinstance(out_shape, (list, tuple))
    return pl.pallas_call(
        kernel,
        out_shape=out_shape,
        in_specs=specs or [VMEM] * len(args),
        out_specs=[VMEM] * len(out_shape) if many else VMEM,
        scratch_shapes=scratch,
        compiler_params=pltpu.CompilerParams(vmem_limit_bytes=limit * 1024 * 1024),
    )(*args)


def f32(*shape):
    return jax.ShapeDtypeStruct(shape, F32)


def ring(axis, step):
    count = lax.axis_size(axis)
    return [(i, (i + step) % count) for i in range(count)]


def lane_iota(rows, lanes=LANES):
    return lax.broadcasted_iota(jnp.int32, (rows, lanes), 1)


def total(values):
    folded = values[:, :LANES]
    for start in range(LANES, values.shape[1], LANES):
        folded = folded + values[:, start : start + LANES]
    return jnp.sum(jnp.sum(folded, axis=0, keepdims=True), axis=1, keepdims=True)


def put(row, lane, value):
    return jnp.where(lane_iota(1) == lane, value, row)


def project(feature, field, columns, brick):
    product = feature * field
    folded = product[:, :LANES]
    for start in range(LANES, product.shape[1], LANES):
        folded = folded + product[:, start : start + LANES]
    column = jnp.sum(folded, axis=1, keepdims=True)
    return jnp.where(lane_iota(columns.shape[0]) == brick, column, columns)


def to_rows(columns, nrows):
    square = jnp.concatenate([columns, jnp.zeros((LANES - columns.shape[0], LANES), F32)], axis=0)
    return square.T[:nrows]


def first_kernel(features, field, neighbours, block, moments, values, ids, buffer, sems):
    nrows, width, _ = features.shape
    each = nrows // CHUNKS
    copies = [
        pltpu.make_async_copy(
            features.at[pl.ds(i * each, each)], buffer.at[pl.ds(i * each, each)], sems.at[i]
        )
        for i in range(CHUNKS)
    ]
    small = [
        pltpu.make_async_copy(field, values, sems.at[CHUNKS]),
        pltpu.make_async_copy(neighbours, ids, sems.at[CHUNKS + 1]),
    ]
    for copy in small + copies[:AHEAD]:
        copy.start()
    for copy in small:
        copy.wait()
    value = values[...]
    moments[...] = put(jnp.zeros((1, LANES), F32), MOMENT_LANE, total(value * value))
    columns = jnp.zeros((width, LANES), F32)
    for i, copy in enumerate(copies):
        copy.wait()
        if i + AHEAD < CHUNKS:
            copies[i + AHEAD].start()
        for b in range(i * each, (i + 1) * each):
            columns = project(buffer[b], values[b : b + 1, :], columns, b)
    block[...] = to_rows(columns, nrows)
    block[:, width : width + neighbours.shape[1]] = ids[...].astype(F32)


def positions(block, nrows, across, row_index, col_index):
    ids = block.astype(jnp.int32)
    owner = lax.shift_right_arithmetic(ids, nrows.bit_length() - 1)
    offset_x = lax.shift_right_arithmetic(owner, across.bit_length() - 1) - row_index + 1
    offset_y = (owner & (across - 1)) - col_index + 1
    inside = (ids >= 0) & (offset_x >= 0) & (offset_x < 3) & (offset_y >= 0) & (offset_y < 3)
    return jnp.where(inside, offset_y * LANES + offset_x * nrows + (ids & (nrows - 1)), -1)


def one_hot(position, first, lanes, width, slots):
    targets = lane_iota(position.shape[0], lanes) + first
    out = jnp.zeros((position.shape[0], lanes), F32)
    for slot in range(width, width + slots):
        out = jnp.where(position[:, slot : slot + 1] == targets, 1.0, out)
    return out.astype(BF16)


def padded(third):
    return jnp.concatenate([third, jnp.zeros((LANES - third.shape[0], third.shape[1]), third.dtype)])


def middle_kernel(shape, index, column, features, out):
    nrows, width, slots, across = shape
    place = positions(column[...], nrows, across, index[0], index[1])
    out[...] = padded(one_hot(place, 0, 3 * LANES, width, slots))


def advance(step, nrows, width, weights, around, features, diagonal, before, sums, moments, outs):
    last = step + 1 == ITERS
    parts = []
    rest = around
    for _ in range(3):
        part = rest.astype(BF16)
        rest = rest - part.astype(F32)
        parts.append(part)
    result = jnp.dot(weights, parts[0], preferred_element_type=F32)
    for part in parts[1:]:
        result = result + jnp.dot(weights, part, preferred_element_type=F32)
    turned = result.T[:width]
    lanes = lane_iota(width)
    shift = step * nrows
    moved = pltpu.roll(turned, shift, 1) if shift else turned
    sums = jnp.where((lanes >= shift) & (lanes < shift + nrows), moved, sums)
    old = before[...]
    base = (diagonal[...] - SHIFT) * old
    columns = jnp.zeros((width, LANES), F32)
    for b in range(nrows):
        second = turned[:, nrows + b : nrows + b + 1]
        image = jnp.sum(features[b] * second, axis=0, keepdims=True)
        new = base[b : b + 1, :] + image
        outs[0][b : b + 1, :] = new
        if not last:
            columns = project(features[b], new, columns, b)
    new = outs[0][...]
    moments = put(moments, MOMENT_LANE + 2 * step + 1, total(old * new))
    if not last:
        moments = put(moments, MOMENT_LANE + 2 * step + 2, total(new * new))
    return sums, moments, columns


def second_kernel(
    shape, index, left, column, right, middle, features, diagonal, before, moments,
    new, block, sums_out, moments_out, weights_out,
):
    nrows, width, slots, across = shape
    own = middle[nrows : 2 * nrows, :]
    pieces = [own[:, d * LANES : (d + 1) * LANES] for d in range(3)]
    centre = middle[...]
    thirds = [jnp.dot(pieces[1], centre[:, d * LANES : (d + 1) * LANES], preferred_element_type=F32) for d in range(3)]
    for d, side in ((0, left), (2, right)):
        place = positions(side[...], nrows, across, index[0], index[1])
        hot = padded(one_hot(place, d * LANES, LANES, width, slots))
        thirds[d] = thirds[d] + jnp.dot(pieces[d], hot, preferred_element_type=F32)
        across_dy = centre[:, d * LANES : (d + 1) * LANES]
        thirds[1] = thirds[1] + lax.dot_general(
            pieces[d], across_dy, (((1,), (1,)), ((), ())), preferred_element_type=F32
        )
    twice = jnp.concatenate(thirds, axis=1).astype(BF16)
    pad = jnp.zeros((LANES - 2 * nrows, 3 * LANES), BF16)
    weights = jnp.concatenate([own, twice, pad], axis=0)
    weights_out[...] = weights
    around = jnp.concatenate([padded(side[...]) for side in (left, column, right)], axis=0)
    sums, moment, columns = advance(
        0, nrows, width, weights, around, features, diagonal, before,
        jnp.zeros((width, LANES), F32), moments[...], [new],
    )
    block[...] = to_rows(columns, nrows)
    sums_out[...] = sums
    moments_out[...] = moment


def third_kernel(
    left, column, right, weights, features, diagonal, before, sums, moments,
    new, block, sums_out, moments_out,
):
    nrows, width, _ = features.shape
    around = jnp.concatenate([padded(side[...]) for side in (left, column, right)], axis=0)
    total_sums, moment, columns = advance(
        1, nrows, width, weights[...], around, features, diagonal, before,
        sums[...], moments[...], [new],
    )
    block[...] = to_rows(columns, nrows)
    sums_out[...] = total_sums
    moments_out[...] = moment


def fourth_kernel(
    left, column, right, weights, features, diagonal, before, sums, moments,
    new, sums_out,
):
    nrows, width, _ = features.shape
    around = jnp.concatenate([padded(side[...]) for side in (left, column, right)], axis=0)
    total_sums, moment, _ = advance(
        2, nrows, width, weights[...], around, features, diagonal, before,
        sums[...], moments[...], [new],
    )
    rows = lax.broadcasted_iota(jnp.int32, total_sums.shape, 0)
    mixed = total_sums + jnp.where(rows == 0, moment, 0.0)
    sums_out[...] = jnp.broadcast_to(mixed[None], sums_out.shape)


def fold_kernel(slab, out):
    row = slab[0, 0:1, :]
    for d in range(1, slab.shape[0]):
        row = row + slab[d, 0:1, :]
    out[...] = jnp.broadcast_to(row, out.shape)


def vertex_values(nrows, index, field, slab, bricks, vertex_features):
    across, width, _ = slab.shape
    local = bricks[...] - index[0] * across * nrows
    hot = lax.broadcasted_iota(jnp.int32, (across * nrows, local.shape[1]), 0) == local
    hot = jnp.where(hot, 1.0, 0.0).astype(BF16)
    group = LANES // nrows
    lanes = lane_iota(width)
    tiles = []
    for start in range(0, across, group):
        tile = jnp.zeros((width, LANES), F32)
        for d in range(group):
            mixed = None
            for k, weight in enumerate(field):
                shift = (d - k) * nrows % LANES
                moved = pltpu.roll(slab[start + d], shift, 1) if shift else slab[start + d]
                mixed = weight * moved if mixed is None else mixed + weight * moved
            tile = jnp.where((lanes >= d * nrows) & (lanes < (d + 1) * nrows), mixed, tile)
        tiles.append(tile)
    rest = jnp.concatenate(tiles, axis=1)
    picked = None
    for _ in range(3):
        part = rest.astype(BF16)
        rest = rest - part.astype(F32)
        value = jnp.dot(part, hot, preferred_element_type=F32)
        picked = value if picked is None else picked + value
    return jnp.sum(vertex_features[...] * picked, axis=0, keepdims=True)


def cg_weights(mu):
    def dot(left, right):
        return sum(left[i] * right[j] * mu[i + j] for i in range(len(left)) for j in range(len(right)))

    def apply(poly):
        out = [SHIFT * p for p in poly] + [0.0]
        for i, p in enumerate(poly):
            out[i + 1] = out[i + 1] + p
        return out

    def axpy(left, scale, right):
        size = max(len(left), len(right))
        left = left + [0.0] * (size - len(left))
        return [l + scale * right[i] if i < len(right) else l for i, l in enumerate(left)]

    field, residual, direction, norm_now = [], [1.0], [1.0], mu[0]
    for step in range(ITERS):
        image = apply(direction)
        alpha = norm_now / dot(direction, image)
        field = axpy(field, alpha, direction)
        residual = axpy(residual, -alpha, image)
        if step + 1 < ITERS:
            norm_next = dot(residual, residual)
            direction = axpy(residual, norm_next / norm_now, direction)
            norm_now = norm_next
    return field, residual


def last_kernel(
    nrows, index, moments, v0, v1, v2, v3, slab, bricks, vertex_features,
    field_out, residual_out, vertices_out,
):
    sums = jnp.sum(moments[...], axis=0, keepdims=True)
    field, residual = cg_weights([sums[:, MOMENT_LANE + i : MOMENT_LANE + i + 1] for i in range(MOMENTS)])
    powers = [v0[...], v1[...], v2[...], v3[...]]
    field_out[...] = sum(w * v for w, v in zip(field, powers))
    residual_out[...] = sum(w * v for w, v in zip(residual, powers))
    vertices_out[...] = vertex_values(nrows, index, field, slab, bricks, vertex_features)


def neighbourhood(block):
    column = jnp.concatenate(
        [lax.ppermute(block, "gx", ring("gx", 1)), block, lax.ppermute(block, "gx", ring("gx", -1))]
    )
    return (
        lax.ppermute(column, "gy", ring("gy", 1)),
        column,
        lax.ppermute(column, "gy", ring("gy", -1)),
    )


def per_device(right_side, diagonal, features, neighbours, vertex_features, vertex_bricks):
    nrows, width, voxels = features.shape
    slots = neighbours.shape[1]
    across, along = lax.axis_size("gy"), lax.axis_size("gx")
    index = jnp.stack([lax.axis_index("gx"), lax.axis_index("gy")]).astype(jnp.int32)
    smem, hbm = pl.BlockSpec(memory_space=pltpu.SMEM), pl.BlockSpec(memory_space=pltpu.HBM)
    shape = (nrows, width, slots, across)
    power = f32(nrows, voxels)
    block_shape, row, table = f32(nrows, LANES), f32(1, LANES), f32(width, LANES)

    block, moments = call(
        first_kernel, [block_shape, row], features, right_side, neighbours,
        specs=[hbm] * 3, limit=FIRST_LIMIT,
        scratch=[
            pltpu.VMEM(right_side.shape, F32),
            pltpu.VMEM(neighbours.shape, jnp.int32),
            pltpu.VMEM(features.shape, F32),
            pltpu.SemaphoreType.DMA((CHUNKS + 2,)),
        ],
    )
    left, column, right = neighbourhood(block)
    middle = call(
        functools.partial(middle_kernel, shape), jax.ShapeDtypeStruct((LANES, 3 * LANES), BF16),
        index, column, features, specs=[smem, VMEM, VMEM],
    )
    v1, block, sums, moments, weights = call(
        functools.partial(second_kernel, shape),
        [power, block_shape, table, row, jax.ShapeDtypeStruct((LANES, 3 * LANES), BF16)],
        index, left, column, right, middle, features, diagonal, right_side, moments,
        specs=[smem] + [VMEM] * 8,
    )
    left, column, right = neighbourhood(block)
    v2, block, sums, moments = call(
        third_kernel, [power, block_shape, table, row],
        left, column, right, weights, features, diagonal, v1, sums, moments,
    )
    left, column, right = neighbourhood(block)
    v3, sums = call(
        fourth_kernel, [power, f32(across, width, LANES)],
        left, column, right, weights, features, diagonal, v2, sums, moments,
    )
    slab = lax.all_to_all(sums, "gy", 0, 0, tiled=True)
    moments = lax.all_to_all(call(fold_kernel, f32(along, LANES), slab), "gx", 0, 0, tiled=True)
    field, residual, values = call(
        functools.partial(last_kernel, nrows), [power, power, f32(1, vertex_bricks.shape[0])],
        index, moments, right_side, v1, v2, v3, slab, vertex_bricks.reshape(1, -1), vertex_features,
        specs=[smem] + [VMEM] * 8,
    )
    return field, residual, values.reshape(-1)


def solution(mesh):
    placed = (
        P(("gx", "gy"), None),
        P(("gx", "gy"), None),
        P(("gx", "gy"), None, None),
        P(("gx", "gy"), None),
        P(None, ("gx", "gy")),
        P(("gx", "gy")),
    )
    return jax.shard_map(
        per_device,
        mesh=mesh,
        in_specs=placed,
        out_specs=(P(("gx", "gy"), None), P(("gx", "gy"), None), P(("gx", "gy"))),
        check_vma=False,
    )
```

```python
import functools

import jax
import jax.numpy as jnp
from jax import lax
from jax.experimental import pallas as pl
from jax.experimental.pallas import tpu as pltpu
from jax.sharding import PartitionSpec as P

ITERS = 3
SHIFT = 1.25
LANES = 128
MOMENTS = 2 * ITERS
CHUNKS = 16
MOMENT_LANE = 96
FIRST_LIMIT = 60
VMEM = pl.BlockSpec(memory_space=pltpu.VMEM)
F32, BF16 = jnp.float32, jnp.bfloat16


def call(kernel, out_shape, *args, specs=None, scratch=(), limit=24):
    many = isinstance(out_shape, (list, tuple))
    return pl.pallas_call(
        kernel,
        out_shape=out_shape,
        in_specs=specs or [VMEM] * len(args),
        out_specs=[VMEM] * len(out_shape) if many else VMEM,
        scratch_shapes=scratch,
        compiler_params=pltpu.CompilerParams(vmem_limit_bytes=limit * 1024 * 1024),
    )(*args)


def f32(*shape):
    return jax.ShapeDtypeStruct(shape, F32)


def ring(axis, step):
    count = lax.axis_size(axis)
    return [(i, (i + step) % count) for i in range(count)]


def lane_iota(rows, lanes=LANES):
    return lax.broadcasted_iota(jnp.int32, (rows, lanes), 1)


def total(values):
    folded = values[:, :LANES]
    for start in range(LANES, values.shape[1], LANES):
        folded = folded + values[:, start : start + LANES]
    return jnp.sum(jnp.sum(folded, axis=0, keepdims=True), axis=1, keepdims=True)


def put(row, lane, value):
    return jnp.where(lane_iota(1) == lane, value, row)


def project(feature, field, columns, brick):
    product = feature * field
    folded = product[:, :LANES]
    for start in range(LANES, product.shape[1], LANES):
        folded = folded + product[:, start : start + LANES]
    column = jnp.sum(folded, axis=1, keepdims=True)
    return jnp.where(lane_iota(columns.shape[0]) == brick, column, columns)


def to_rows(columns, nrows):
    square = jnp.concatenate([columns, jnp.zeros((LANES - columns.shape[0], LANES), F32)], axis=0)
    return square.T[:nrows]


def first_kernel(features, field, neighbours, block, moments, values, ids, buffer, sems):
    nrows, width, _ = features.shape
    each = nrows // CHUNKS
    copies = [
        pltpu.make_async_copy(
            features.at[pl.ds(i * each, each)], buffer.at[pl.ds(i * each, each)], sems.at[i]
        )
        for i in range(CHUNKS)
    ]
    small = [
        pltpu.make_async_copy(field, values, sems.at[CHUNKS]),
        pltpu.make_async_copy(neighbours, ids, sems.at[CHUNKS + 1]),
    ]
    for copy in small + copies:
        copy.start()
    for copy in small:
        copy.wait()
    value = values[...]
    moments[...] = put(jnp.zeros((1, LANES), F32), MOMENT_LANE, total(value * value))
    columns = jnp.zeros((width, LANES), F32)
    for i, copy in enumerate(copies):
        copy.wait()
        for b in range(i * each, (i + 1) * each):
            columns = project(buffer[b], values[b : b + 1, :], columns, b)
    block[...] = to_rows(columns, nrows)
    block[:, width : width + neighbours.shape[1]] = ids[...].astype(F32)


def positions(block, nrows, across, row_index, col_index):
    ids = block.astype(jnp.int32)
    owner = lax.shift_right_arithmetic(ids, nrows.bit_length() - 1)
    offset_x = lax.shift_right_arithmetic(owner, across.bit_length() - 1) - row_index + 1
    offset_y = (owner & (across - 1)) - col_index + 1
    inside = (ids >= 0) & (offset_x >= 0) & (offset_x < 3) & (offset_y >= 0) & (offset_y < 3)
    return jnp.where(inside, offset_y * LANES + offset_x * nrows + (ids & (nrows - 1)), -1)


def one_hot(position, first, lanes, width, slots):
    targets = lane_iota(position.shape[0], lanes) + first
    out = jnp.zeros((position.shape[0], lanes), F32)
    for slot in range(width, width + slots):
        out = jnp.where(position[:, slot : slot + 1] == targets, 1.0, out)
    return out.astype(BF16)


def padded(third):
    return jnp.concatenate([third, jnp.zeros((LANES - third.shape[0], third.shape[1]), third.dtype)])


def third_of(table, d):
    return table[:, d * LANES : (d + 1) * LANES]


def own_kernel(shape, index, block, features, own, copy):
    nrows, width, slots, across = shape
    copy[...] = block[...]
    place = positions(block[...], nrows, across, index[0], index[1])
    own[...] = one_hot(place, 0, 3 * LANES, width, slots)


def middle_kernel(shape, index, column, own, twice):
    nrows, width, slots, across = shape
    others = jnp.concatenate([column[:nrows, :], column[2 * nrows :, :]], axis=0)
    place = positions(others, nrows, across, index[0], index[1])
    hot = one_hot(place, 0, 3 * LANES, width, slots)
    mine = own[...]
    centre = padded(jnp.concatenate([hot[:nrows], mine, hot[nrows:]], axis=0))
    known = jnp.dot(third_of(mine, 1), centre, preferred_element_type=F32)
    extra = [
        lax.dot_general(
            third_of(mine, d), third_of(centre, d), (((1,), (1,)), ((), ())), preferred_element_type=F32
        )
        for d in (0, 2)
    ]
    parts = [third_of(known, 0), third_of(known, 1) + extra[0] + extra[1], third_of(known, 2)]
    twice[...] = jnp.concatenate(parts, axis=1)


def advance(step, nrows, width, weights, around, features, diagonal, before, sums, moments, outs):
    last = step + 1 == ITERS
    parts = []
    rest = around
    for _ in range(3):
        part = rest.astype(BF16)
        rest = rest - part.astype(F32)
        parts.append(part)
    result = jnp.dot(weights, parts[0], preferred_element_type=F32)
    for part in parts[1:]:
        result = result + jnp.dot(weights, part, preferred_element_type=F32)
    turned = result.T[:width]
    lanes = lane_iota(width)
    shift = step * nrows
    moved = pltpu.roll(turned, shift, 1) if shift else turned
    sums = jnp.where((lanes >= shift) & (lanes < shift + nrows), moved, sums)
    old = before[...]
    images = [
        jnp.sum(features[b] * turned[:, nrows + b : nrows + b + 1], axis=0, keepdims=True)
        for b in range(nrows)
    ]
    new = (diagonal[...] - SHIFT) * old + jnp.concatenate(images, axis=0)
    outs[0][...] = new
    columns = jnp.zeros((width, LANES), F32)
    if not last:
        for b in range(nrows):
            columns = project(features[b], outs[0][b : b + 1, :], columns, b)
    moments = put(moments, MOMENT_LANE + 2 * step + 1, total(old * new))
    if not last:
        moments = put(moments, MOMENT_LANE + 2 * step + 2, total(new * new))
    return sums, moments, columns


def second_kernel(
    shape, index, left, column, right, own, known, features, diagonal, before, moments,
    new, block, sums_out, moments_out, weights_out,
):
    nrows, width, slots, across = shape
    mine = own[...]
    thirds = [third_of(known, d) for d in range(3)]
    for d, side in ((0, left), (2, right)):
        place = positions(side[...], nrows, across, index[0], index[1])
        hot = padded(one_hot(place, d * LANES, LANES, width, slots))
        thirds[d] = thirds[d] + jnp.dot(third_of(mine, d), hot, preferred_element_type=F32)
    twice = jnp.concatenate(thirds, axis=1).astype(BF16)
    pad = jnp.zeros((LANES - 2 * nrows, 3 * LANES), BF16)
    weights = jnp.concatenate([mine, twice, pad], axis=0)
    weights_out[...] = weights
    around = jnp.concatenate([padded(side[...]) for side in (left, column, right)], axis=0)
    sums, moment, columns = advance(
        0, nrows, width, weights, around, features, diagonal, before,
        jnp.zeros((width, LANES), F32), moments[...], [new],
    )
    block[...] = to_rows(columns, nrows)
    sums_out[...] = sums
    moments_out[...] = moment


def third_kernel(
    left, column, right, weights, features, diagonal, before, sums, moments,
    new, block, sums_out, moments_out,
):
    nrows, width, _ = features.shape
    around = jnp.concatenate([padded(side[...]) for side in (left, column, right)], axis=0)
    total_sums, moment, columns = advance(
        1, nrows, width, weights[...], around, features, diagonal, before,
        sums[...], moments[...], [new],
    )
    block[...] = to_rows(columns, nrows)
    sums_out[...] = total_sums
    moments_out[...] = moment


def fourth_kernel(
    left, column, right, weights, features, diagonal, before, sums, moments,
    new, sums_out,
):
    nrows, width, _ = features.shape
    around = jnp.concatenate([padded(side[...]) for side in (left, column, right)], axis=0)
    total_sums, moment, _ = advance(
        2, nrows, width, weights[...], around, features, diagonal, before,
        sums[...], moments[...], [new],
    )
    rows = lax.broadcasted_iota(jnp.int32, total_sums.shape, 0)
    mixed = total_sums + jnp.where(rows == 0, moment, 0.0)
    sums_out[...] = jnp.broadcast_to(mixed[None], sums_out.shape)


def fold_kernel(slab, out):
    row = slab[0, 0:1, :]
    for d in range(1, slab.shape[0]):
        row = row + slab[d, 0:1, :]
    out[...] = jnp.broadcast_to(row, out.shape)


def vertex_kernel(nrows, index, slab, bricks, vertex_features, out):
    across, width, _ = slab.shape
    local = bricks[...] - index[0] * across * nrows
    hot = lax.broadcasted_iota(jnp.int32, (across * nrows, local.shape[1]), 0) == local
    hot = jnp.where(hot, 1.0, 0.0).astype(BF16)
    group = LANES // nrows
    lanes = lane_iota(width)
    table = []
    for k in range(ITERS):
        tiles = []
        for start in range(0, across, group):
            tile = jnp.zeros((width, LANES), F32)
            for d in range(group):
                shift = (d - k) * nrows % LANES
                moved = pltpu.roll(slab[start + d], shift, 1) if shift else slab[start + d]
                tile = jnp.where((lanes >= d * nrows) & (lanes < (d + 1) * nrows), moved, tile)
            tiles.append(tile)
        table.append(jnp.concatenate(tiles, axis=1))
    rest = jnp.concatenate(table, axis=0)
    picked = None
    for _ in range(3):
        part = rest.astype(BF16)
        rest = rest - part.astype(F32)
        value = jnp.dot(part, hot, preferred_element_type=F32)
        picked = value if picked is None else picked + value
    for k in range(ITERS):
        product = vertex_features[...] * picked[k * width : (k + 1) * width, :]
        out[k : k + 1, :] = jnp.sum(product, axis=0, keepdims=True)


def cg_weights(mu):
    def dot(left, right):
        return sum(left[i] * right[j] * mu[i + j] for i in range(len(left)) for j in range(len(right)))

    def apply(poly):
        out = [SHIFT * p for p in poly] + [0.0]
        for i, p in enumerate(poly):
            out[i + 1] = out[i + 1] + p
        return out

    def axpy(left, scale, right):
        size = max(len(left), len(right))
        left = left + [0.0] * (size - len(left))
        return [l + scale * right[i] if i < len(right) else l for i, l in enumerate(left)]

    field, residual, direction, norm_now = [], [1.0], [1.0], mu[0]
    for step in range(ITERS):
        image = apply(direction)
        alpha = norm_now / dot(direction, image)
        field = axpy(field, alpha, direction)
        residual = axpy(residual, -alpha, image)
        if step + 1 < ITERS:
            norm_next = dot(residual, residual)
            direction = axpy(residual, norm_next / norm_now, direction)
            norm_now = norm_next
    return field, residual


def last_kernel(moments, v0, v1, v2, v3, vertices, field_out, residual_out, vertices_out):
    sums = jnp.sum(moments[...], axis=0, keepdims=True)
    field, residual = cg_weights([sums[:, MOMENT_LANE + i : MOMENT_LANE + i + 1] for i in range(MOMENTS)])
    powers = [v0[...], v1[...], v2[...], v3[...]]
    field_out[...] = sum(w * v for w, v in zip(field, powers))
    residual_out[...] = sum(w * v for w, v in zip(residual, powers))
    vertices_out[...] = sum(w * vertices[i : i + 1, :] for i, w in enumerate(field))


def neighbourhood(block, copy=None):
    up, down = lax.ppermute(block, "gx", ring("gx", 1)), lax.ppermute(block, "gx", ring("gx", -1))
    column = jnp.concatenate([up, block if copy is None else copy, down])
    return (
        lax.ppermute(column, "gy", ring("gy", 1)),
        column,
        lax.ppermute(column, "gy", ring("gy", -1)),
    )


def per_device(right_side, diagonal, features, neighbours, vertex_features, vertex_bricks):
    nrows, width, voxels = features.shape
    slots = neighbours.shape[1]
    across, along = lax.axis_size("gy"), lax.axis_size("gx")
    index = jnp.stack([lax.axis_index("gx"), lax.axis_index("gy")]).astype(jnp.int32)
    smem, hbm = pl.BlockSpec(memory_space=pltpu.SMEM), pl.BlockSpec(memory_space=pltpu.HBM)
    shape = (nrows, width, slots, across)
    power = f32(nrows, voxels)
    block_shape, row, table = f32(nrows, LANES), f32(1, LANES), f32(width, LANES)

    block, moments = call(
        first_kernel, [block_shape, row], features, right_side, neighbours,
        specs=[hbm] * 3, limit=FIRST_LIMIT,
        scratch=[
            pltpu.VMEM(right_side.shape, F32),
            pltpu.VMEM(neighbours.shape, jnp.int32),
            pltpu.VMEM(features.shape, F32),
            pltpu.SemaphoreType.DMA((CHUNKS + 2,)),
        ],
    )
    own, copy = call(
        functools.partial(own_kernel, shape),
        [jax.ShapeDtypeStruct((nrows, 3 * LANES), BF16), block_shape],
        index, block, features, specs=[smem, VMEM, VMEM],
    )
    left, column, right = neighbourhood(block, copy)
    known = call(
        functools.partial(middle_kernel, shape), f32(nrows, 3 * LANES),
        index, column, own, specs=[smem, VMEM, VMEM],
    )
    v1, block, sums, moments, weights = call(
        functools.partial(second_kernel, shape),
        [power, block_shape, table, row, jax.ShapeDtypeStruct((LANES, 3 * LANES), BF16)],
        index, left, column, right, own, known, features, diagonal, right_side, moments,
        specs=[smem] + [VMEM] * 9,
    )
    left, column, right = neighbourhood(block)
    v2, block, sums, moments = call(
        third_kernel, [power, block_shape, table, row],
        left, column, right, weights, features, diagonal, v1, sums, moments,
    )
    left, column, right = neighbourhood(block)
    v3, sums = call(
        fourth_kernel, [power, f32(across, width, LANES)],
        left, column, right, weights, features, diagonal, v2, sums, moments,
    )
    slab = lax.all_to_all(sums, "gy", 0, 0, tiled=True)
    moments = lax.all_to_all(call(fold_kernel, f32(along, LANES), slab), "gx", 0, 0, tiled=True)
    vertices = call(
        functools.partial(vertex_kernel, nrows), f32(8, vertex_bricks.shape[0]),
        index, slab, vertex_bricks.reshape(1, -1), vertex_features, specs=[smem] + [VMEM] * 3,
    )
    field, residual, values = call(
        last_kernel, [power, power, f32(1, vertex_bricks.shape[0])],
        moments, right_side, v1, v2, v3, vertices,
    )
    return field, residual, values.reshape(-1)


def solution(mesh):
    placed = (
        P(("gx", "gy"), None),
        P(("gx", "gy"), None),
        P(("gx", "gy"), None, None),
        P(("gx", "gy"), None),
        P(None, ("gx", "gy")),
        P(("gx", "gy")),
    )
    return jax.shard_map(
        per_device,
        mesh=mesh,
        in_specs=placed,
        out_specs=(P(("gx", "gy"), None), P(("gx", "gy"), None), P(("gx", "gy"))),
        check_vma=False,
    )
```

```python
import functools

import jax
import jax.numpy as jnp
from jax import lax
from jax.experimental import pallas as pl
from jax.experimental.pallas import tpu as pltpu
from jax.sharding import PartitionSpec as P

ITERS = 3
SHIFT = 1.25
LANES = 128
MOMENTS = 2 * ITERS
CHUNKS = 16
MOMENT_LANE = 96
FIRST_LIMIT = 60
VMEM = pl.BlockSpec(memory_space=pltpu.VMEM)
F32, BF16 = jnp.float32, jnp.bfloat16


def call(kernel, out_shape, *args, specs=None, scratch=(), limit=12):
    many = isinstance(out_shape, (list, tuple))
    return pl.pallas_call(
        kernel,
        out_shape=out_shape,
        in_specs=specs or [VMEM] * len(args),
        out_specs=[VMEM] * len(out_shape) if many else VMEM,
        scratch_shapes=scratch,
        compiler_params=pltpu.CompilerParams(vmem_limit_bytes=limit * 1024 * 1024),
    )(*args)


def f32(*shape):
    return jax.ShapeDtypeStruct(shape, F32)


def ring(axis, step):
    count = lax.axis_size(axis)
    return [(i, (i + step) % count) for i in range(count)]


def lane_iota(rows, lanes=LANES):
    return lax.broadcasted_iota(jnp.int32, (rows, lanes), 1)


def total(values):
    folded = values[:, :LANES]
    for start in range(LANES, values.shape[1], LANES):
        folded = folded + values[:, start : start + LANES]
    return jnp.sum(jnp.sum(folded, axis=0, keepdims=True), axis=1, keepdims=True)


def put(row, lane, value):
    return jnp.where(lane_iota(1) == lane, value, row)


def project(feature, field, columns, brick):
    product = feature * field
    folded = product[:, :LANES]
    for start in range(LANES, product.shape[1], LANES):
        folded = folded + product[:, start : start + LANES]
    column = jnp.sum(folded, axis=1, keepdims=True)
    return jnp.where(lane_iota(columns.shape[0]) == brick, column, columns)


def to_rows(columns, nrows):
    square = jnp.concatenate([columns, jnp.zeros((LANES - columns.shape[0], LANES), F32)], axis=0)
    return square.T[:nrows]


def first_kernel(features, field, neighbours, block, moments, values, ids, buffer, sems):
    nrows, width, _ = features.shape
    each = nrows // CHUNKS
    copies = [
        pltpu.make_async_copy(
            features.at[pl.ds(i * each, each)], buffer.at[pl.ds(i * each, each)], sems.at[i]
        )
        for i in range(CHUNKS)
    ]
    small = [
        pltpu.make_async_copy(field, values, sems.at[CHUNKS]),
        pltpu.make_async_copy(neighbours, ids, sems.at[CHUNKS + 1]),
    ]
    for copy in small + copies:
        copy.start()
    for copy in small:
        copy.wait()
    value = values[...]
    moments[...] = put(jnp.zeros((1, LANES), F32), MOMENT_LANE, total(value * value))
    columns = jnp.zeros((width, LANES), F32)
    for i, copy in enumerate(copies):
        copy.wait()
        for b in range(i * each, (i + 1) * each):
            columns = project(buffer[b], values[b : b + 1, :], columns, b)
    block[...] = to_rows(columns, nrows)
    block[:, width : width + neighbours.shape[1]] = ids[...].astype(F32)


def positions(block, nrows, across, row_index, col_index):
    ids = block.astype(jnp.int32)
    owner = lax.shift_right_arithmetic(ids, nrows.bit_length() - 1)
    offset_x = lax.shift_right_arithmetic(owner, across.bit_length() - 1) - row_index + 1
    offset_y = (owner & (across - 1)) - col_index + 1
    inside = (ids >= 0) & (offset_x >= 0) & (offset_x < 3) & (offset_y >= 0) & (offset_y < 3)
    return jnp.where(inside, offset_y * LANES + offset_x * nrows + (ids & (nrows - 1)), -1)


def one_hot(position, first, lanes, width, slots):
    targets = lane_iota(position.shape[0], lanes) + first
    out = jnp.zeros((position.shape[0], lanes), F32)
    for slot in range(width, width + slots):
        out = jnp.where(position[:, slot : slot + 1] == targets, 1.0, out)
    return out.astype(BF16)


def padded(third):
    return jnp.concatenate([third, jnp.zeros((LANES - third.shape[0], third.shape[1]), third.dtype)])


def third_of(table, d):
    return table[:, d * LANES : (d + 1) * LANES]


def own_kernel(shape, index, block, features, own, copy):
    nrows, width, slots, across = shape
    copy[...] = block[...]
    place = positions(block[...], nrows, across, index[0], index[1])
    own[...] = one_hot(place, 0, 3 * LANES, width, slots)


def middle_kernel(shape, index, column, own, twice):
    nrows, width, slots, across = shape
    others = jnp.concatenate([column[:nrows, :], column[2 * nrows :, :]], axis=0)
    place = positions(others, nrows, across, index[0], index[1])
    hot = one_hot(place, 0, 3 * LANES, width, slots)
    mine = own[...]
    centre = padded(jnp.concatenate([hot[:nrows], mine, hot[nrows:]], axis=0))
    known = jnp.dot(third_of(mine, 1), centre, preferred_element_type=F32)
    extra = [
        lax.dot_general(
            third_of(mine, d), third_of(centre, d), (((1,), (1,)), ((), ())), preferred_element_type=F32
        )
        for d in (0, 2)
    ]
    parts = [third_of(known, 0), third_of(known, 1) + extra[0] + extra[1], third_of(known, 2)]
    twice[...] = jnp.concatenate(parts, axis=1)


def products(weights, values):
    result, rest = None, values
    for _ in range(3):
        part = rest.astype(BF16)
        rest = rest - part.astype(F32)
        value = jnp.dot(weights, part, preferred_element_type=F32)
        result = value if result is None else result + value
    return result


def expand(result, nrows, features, shifted, old):
    turned = result.T[: features.shape[1]]
    images = [
        jnp.sum(features[b] * turned[:, nrows + b : nrows + b + 1], axis=0, keepdims=True)
        for b in range(nrows)
    ]
    return shifted * old + jnp.concatenate(images, axis=0)


def advance(step, weights, around, features, diagonal, before, moments, new, sums, block):
    nrows, width, _ = features.shape
    result = products(weights, around)
    sums[...] = result[:nrows]
    old, shifted = before[...], diagonal[...] - SHIFT
    value = expand(result, nrows, features, shifted, old)
    new[...] = value
    columns = jnp.zeros((width, LANES), F32)
    for b in range(nrows):
        columns = project(features[b], new[b : b + 1, :], columns, b)
    block[...] = to_rows(columns, nrows)
    moments = put(moments, MOMENT_LANE + 2 * step + 1, total(old * value))
    moments = put(moments, MOMENT_LANE + 2 * step + 2, total(value * value))
    if step + 2 == ITERS:
        moments = put(moments, MOMENT_LANE + 2 * step + 3, total(value * value * shifted))
    return moments


def second_kernel(
    shape, index, left, column, right, own, known, features, diagonal, before, moments,
    new, block, sums, moments_out, weights_out, tables,
):
    nrows, width, slots, across = shape
    mine = own[...]
    thirds = [third_of(known, d) for d in range(3)]
    for d, side in ((0, left), (2, right)):
        place = positions(side[...], nrows, across, index[0], index[1])
        hot = padded(one_hot(place, d * LANES, LANES, width, slots))
        thirds[d] = thirds[d] + jnp.dot(third_of(mine, d), hot, preferred_element_type=F32)
    twice = jnp.concatenate(thirds, axis=1).astype(BF16)
    pad = jnp.zeros((LANES - 2 * nrows, 3 * LANES), BF16)
    weights = jnp.concatenate([mine, twice, pad], axis=0)
    weights_out[...] = weights
    tables[...] = jnp.concatenate([side[nrows : 2 * nrows, :] for side in (left, column, right)], axis=0)
    around = jnp.concatenate([padded(side[...]) for side in (left, column, right)], axis=0)
    moments_out[...] = advance(
        0, weights, around, features, diagonal, before, moments[...], new, sums, block
    )


def third_kernel(
    left, column, right, weights, features, diagonal, before, moments, far, ahead,
    new, block, sums, moments_out,
):
    around = jnp.concatenate([padded(side[...]) for side in (left, column, right)], axis=0)
    moments_out[...] = advance(
        1, weights[...], around, features, diagonal, before, moments[...], new, sums, block
    )


def slab_hot_kernel(shape, index, far, near, ahead, block, out, ids):
    nrows, width, slots, across = shape
    for j in range(across):
        source, part = ((far, j), (near, j - 3), (ahead, j - 6))[j // 3]
        ids[j] = source[part * nrows : (part + 1) * nrows, :]
    span = 3 * nrows
    for a in range(across):
        table = ids[(a - index[1] + across // 2) & (across - 1)].astype(jnp.int32)
        owner = lax.shift_right_arithmetic(table, nrows.bit_length() - 1)
        offset_x = lax.shift_right_arithmetic(owner, across.bit_length() - 1) - index[0] + 1
        place = (owner & (across - 1)) * span + offset_x * nrows + (table & (nrows - 1))
        place = jnp.where((table >= 0) & (offset_x >= 0) & (offset_x < 3), place, -1)
        first = max(a - 1, 0) * span // LANES * LANES
        last = -(-min(a + 2, across) * span // LANES) * LANES
        rows = pl.ds(a * nrows, nrows)
        if first:
            out[rows, :first] = jnp.zeros((nrows, first), BF16)
        out[rows, first:last] = one_hot(place, first, last - first, width, slots)
        if last < out.shape[1]:
            out[rows, last:] = jnp.zeros((nrows, out.shape[1] - last), BF16)


def pack_kernel(up, block, down, first_sums, second_sums, moments, hot, out):
    nrows = block.shape[0]
    low = lane_iota(nrows) < LANES // 2
    top = lax.broadcasted_iota(jnp.int32, (nrows, LANES), 0) == 0
    parts = [
        jnp.where(low, up[...], pltpu.roll(first_sums[...], LANES // 2, 1)),
        jnp.where(low, block[...], pltpu.roll(second_sums[...], LANES // 2, 1)),
        jnp.where(low, down[...], jnp.where(top, moments[...], 0.0)),
    ]
    out[...] = jnp.broadcast_to(jnp.concatenate(parts, axis=0)[None], out.shape)


def slab_kernel(hot, slab, sums, out):
    across, span, _ = slab.shape
    result = products(hot[...], jnp.concatenate([slab[d] for d in range(across)], axis=0))
    sums[...] = result
    start = span // 3 * 2
    row = slab[0, start : start + 1, :]
    for d in range(1, across):
        row = row + slab[d, start : start + 1, :]
    square = total(jnp.where(lane_iota(result.shape[0]) < LANES // 2, result * result, 0.0))
    row = jnp.where(lane_iota(1) == MOMENT_LANE + MOMENTS - 1, row + square, row)
    out[...] = jnp.broadcast_to(row, out.shape)


def fourth_kernel(index, slab, weights, features, diagonal, before, new):
    across = slab.shape[0]
    around = [padded(slab[(index[1] + d) & (across - 1)]) for d in (across - 1, 0, 1)]
    result = products(weights[...], jnp.concatenate(around, axis=0))
    new[...] = expand(result, features.shape[0], features, diagonal[...] - SHIFT, before[...])


def vertex_kernel(nrows, index, slab, sums, bricks, vertex_features, out):
    across, _, _ = slab.shape
    width = vertex_features.shape[0]
    local = bricks[...] - index[0] * across * nrows
    hot = lax.broadcasted_iota(jnp.int32, (across * nrows, local.shape[1]), 0) == local
    hot = jnp.where(hot, 1.0, 0.0).astype(BF16)
    table = [
        jnp.concatenate([slab[d, k * nrows : (k + 1) * nrows, :] for d in range(across)], axis=0).T[width:]
        for k in range(2)
    ]
    rest = jnp.concatenate(table + [sums[...].T[:width]], axis=0)
    picked = None
    for _ in range(3):
        part = rest.astype(BF16)
        rest = rest - part.astype(F32)
        value = jnp.dot(part, hot, preferred_element_type=F32)
        picked = value if picked is None else picked + value
    for k in range(ITERS):
        product = vertex_features[...] * picked[k * width : (k + 1) * width, :]
        out[k : k + 1, :] = jnp.sum(product, axis=0, keepdims=True)


def cg_weights(mu):
    def dot(left, right):
        return sum(left[i] * right[j] * mu[i + j] for i in range(len(left)) for j in range(len(right)))

    def apply(poly):
        out = [SHIFT * p for p in poly] + [0.0]
        for i, p in enumerate(poly):
            out[i + 1] = out[i + 1] + p
        return out

    def axpy(left, scale, right):
        size = max(len(left), len(right))
        left = left + [0.0] * (size - len(left))
        return [l + scale * right[i] if i < len(right) else l for i, l in enumerate(left)]

    field, residual, direction, norm_now = [], [1.0], [1.0], mu[0]
    for step in range(ITERS):
        image = apply(direction)
        alpha = norm_now / dot(direction, image)
        field = axpy(field, alpha, direction)
        residual = axpy(residual, -alpha, image)
        if step + 1 < ITERS:
            norm_next = dot(residual, residual)
            direction = axpy(residual, norm_next / norm_now, direction)
            norm_now = norm_next
    return field, residual


def last_kernel(moments, v0, v1, v2, v3, vertices, field_out, residual_out, vertices_out):
    sums = jnp.sum(moments[...], axis=0, keepdims=True)
    field, residual = cg_weights([sums[:, MOMENT_LANE + i : MOMENT_LANE + i + 1] for i in range(MOMENTS)])
    powers = [v0[...], v1[...], v2[...], v3[...]]
    field_out[...] = sum(w * v for w, v in zip(field, powers))
    residual_out[...] = sum(w * v for w, v in zip(residual, powers))
    vertices_out[...] = sum(w * vertices[i : i + 1, :] for i, w in enumerate(field))


def neighbourhood(block, copy=None):
    up, down = lax.ppermute(block, "gx", ring("gx", 1)), lax.ppermute(block, "gx", ring("gx", -1))
    column = jnp.concatenate([up, block if copy is None else copy, down])
    return (
        lax.ppermute(column, "gy", ring("gy", 1)),
        column,
        lax.ppermute(column, "gy", ring("gy", -1)),
    )


def per_device(right_side, diagonal, features, neighbours, vertex_features, vertex_bricks):
    nrows, width, voxels = features.shape
    slots = neighbours.shape[1]
    across, along = lax.axis_size("gy"), lax.axis_size("gx")
    index = jnp.stack([lax.axis_index("gx"), lax.axis_index("gy")]).astype(jnp.int32)
    smem, hbm = pl.BlockSpec(memory_space=pltpu.SMEM), pl.BlockSpec(memory_space=pltpu.HBM)
    shape = (nrows, width, slots, across)
    power = f32(nrows, voxels)
    block_shape, row = f32(nrows, LANES), f32(1, LANES)

    block, moments = call(
        first_kernel, [block_shape, row], features, right_side, neighbours,
        specs=[hbm] * 3, limit=FIRST_LIMIT,
        scratch=[
            pltpu.VMEM(right_side.shape, F32),
            pltpu.VMEM(neighbours.shape, jnp.int32),
            pltpu.VMEM(features.shape, F32),
            pltpu.SemaphoreType.DMA((CHUNKS + 2,)),
        ],
    )
    own, copy = call(
        functools.partial(own_kernel, shape),
        [jax.ShapeDtypeStruct((nrows, 3 * LANES), BF16), block_shape],
        index, block, features, specs=[smem, VMEM, VMEM],
    )
    left, column, right = neighbourhood(block, copy)
    known = call(
        functools.partial(middle_kernel, shape), f32(nrows, 3 * LANES),
        index, column, own, specs=[smem, VMEM, VMEM],
    )
    tables_shape = f32(3 * nrows, LANES)
    v1, block, first_sums, moments, weights, tables = call(
        functools.partial(second_kernel, shape),
        [power, block_shape, block_shape, row, jax.ShapeDtypeStruct((LANES, 3 * LANES), BF16), tables_shape],
        index, left, column, right, own, known, features, diagonal, right_side, moments,
        specs=[smem] + [VMEM] * 9,
    )
    left, column, right = neighbourhood(block)
    far = lax.ppermute(tables, "gy", ring("gy", 3))
    ahead = lax.ppermute(tables, "gy", ring("gy", -3))
    v2, block, second_sums, moments = call(
        third_kernel, [power, block_shape, block_shape, row],
        left, column, right, weights, features, diagonal, v1, moments, far, ahead,
    )
    up, down = lax.ppermute(block, "gx", ring("gx", 1)), lax.ppermute(block, "gx", ring("gx", -1))
    hot = call(
        functools.partial(slab_hot_kernel, shape),
        jax.ShapeDtypeStruct((across * nrows, across * 3 * nrows), BF16),
        index, far, tables, ahead, block, specs=[smem] + [VMEM] * 4,
        scratch=[pltpu.VMEM((across, nrows, LANES), F32)],
    )
    packed = call(
        pack_kernel, f32(across, 3 * nrows, LANES),
        up, block, down, first_sums, second_sums, moments, hot,
    )
    slab = lax.all_to_all(packed, "gy", 0, 0, tiled=True)
    sums, moments = call(slab_kernel, [f32(across * nrows, LANES), f32(along, LANES)], hot, slab)
    moments = lax.all_to_all(moments, "gx", 0, 0, tiled=True)
    v3 = call(
        fourth_kernel, power, index, slab, weights, features, diagonal, v2,
        specs=[smem] + [VMEM] * 5,
    )
    vertices = call(
        functools.partial(vertex_kernel, nrows), f32(8, vertex_bricks.shape[0]),
        index, slab, sums, vertex_bricks.reshape(1, -1), vertex_features, specs=[smem] + [VMEM] * 4,
    )
    field, residual, values = call(
        last_kernel, [power, power, f32(1, vertex_bricks.shape[0])],
        moments, right_side, v1, v2, v3, vertices,
    )
    return field, residual, values.reshape(-1)


def solution(mesh):
    placed = (
        P(("gx", "gy"), None),
        P(("gx", "gy"), None),
        P(("gx", "gy"), None, None),
        P(("gx", "gy"), None),
        P(None, ("gx", "gy")),
        P(("gx", "gy")),
    )
    return jax.shard_map(
        per_device,
        mesh=mesh,
        in_specs=placed,
        out_specs=(P(("gx", "gy"), None), P(("gx", "gy"), None), P(("gx", "gy"))),
        check_vma=False,
    )
```

```python
import functools

import jax
import jax.numpy as jnp
from jax import lax
from jax.experimental import pallas as pl
from jax.experimental.pallas import tpu as pltpu
from jax.sharding import PartitionSpec as P

ITERS = 3
SHIFT = 1.25
LANES = 128
MOMENTS = 2 * ITERS
CHUNKS = 16
MOMENT_LANE = 96
FIRST_LIMIT = 60
VMEM = pl.BlockSpec(memory_space=pltpu.VMEM)
F32, BF16 = jnp.float32, jnp.bfloat16


def call(kernel, out_shape, *args, specs=None, scratch=(), limit=12):
    many = isinstance(out_shape, (list, tuple))
    return pl.pallas_call(
        kernel,
        out_shape=out_shape,
        in_specs=specs or [VMEM] * len(args),
        out_specs=[VMEM] * len(out_shape) if many else VMEM,
        scratch_shapes=scratch,
        compiler_params=pltpu.CompilerParams(vmem_limit_bytes=limit * 1024 * 1024),
    )(*args)


def f32(*shape):
    return jax.ShapeDtypeStruct(shape, F32)


def ring(axis, step):
    count = lax.axis_size(axis)
    return [(i, (i + step) % count) for i in range(count)]


def lane_iota(rows, lanes=LANES):
    return lax.broadcasted_iota(jnp.int32, (rows, lanes), 1)


def total(values):
    folded = values[:, :LANES]
    for start in range(LANES, values.shape[1], LANES):
        folded = folded + values[:, start : start + LANES]
    return jnp.sum(jnp.sum(folded, axis=0, keepdims=True), axis=1, keepdims=True)


def put(row, lane, value):
    return jnp.where(lane_iota(1) == lane, value, row)


def project(feature, field, columns, brick):
    product = feature * field
    folded = product[:, :LANES]
    for start in range(LANES, product.shape[1], LANES):
        folded = folded + product[:, start : start + LANES]
    column = jnp.sum(folded, axis=1, keepdims=True)
    return jnp.where(lane_iota(columns.shape[0]) == brick, column, columns)


def to_rows(columns, nrows):
    square = jnp.concatenate([columns, jnp.zeros((LANES - columns.shape[0], LANES), F32)], axis=0)
    return square.T[:nrows]


def first_kernel(features, field, neighbours, block, moments, values, ids, buffer, sems):
    nrows, width, _ = features.shape
    each = nrows // CHUNKS
    copies = [
        pltpu.make_async_copy(
            features.at[pl.ds(i * each, each)], buffer.at[pl.ds(i * each, each)], sems.at[i]
        )
        for i in range(CHUNKS)
    ]
    small = [
        pltpu.make_async_copy(field, values, sems.at[CHUNKS]),
        pltpu.make_async_copy(neighbours, ids, sems.at[CHUNKS + 1]),
    ]
    for copy in small + copies:
        copy.start()
    for copy in small:
        copy.wait()
    value = values[...]
    moments[...] = put(jnp.zeros((1, LANES), F32), MOMENT_LANE, total(value * value))
    columns = jnp.zeros((width, LANES), F32)
    for i, copy in enumerate(copies):
        copy.wait()
        for b in range(i * each, (i + 1) * each):
            columns = project(buffer[b], values[b : b + 1, :], columns, b)
    block[...] = to_rows(columns, nrows)
    block[:, width : width + neighbours.shape[1]] = ids[...].astype(F32)


def positions(block, nrows, across, row_index, col_index):
    ids = block.astype(jnp.int32)
    owner = lax.shift_right_arithmetic(ids, nrows.bit_length() - 1)
    offset_x = lax.shift_right_arithmetic(owner, across.bit_length() - 1) - row_index + 1
    offset_y = (owner & (across - 1)) - col_index + 1
    inside = (ids >= 0) & (offset_x >= 0) & (offset_x < 3) & (offset_y >= 0) & (offset_y < 3)
    return jnp.where(inside, offset_y * LANES + offset_x * nrows + (ids & (nrows - 1)), -1)


def one_hot(position, first, lanes, width, slots):
    targets = lane_iota(position.shape[0], lanes) + first
    out = jnp.zeros((position.shape[0], lanes), F32)
    for slot in range(width, width + slots):
        out = jnp.where(position[:, slot : slot + 1] == targets, 1.0, out)
    return out.astype(BF16)


def padded(third):
    return jnp.concatenate([third, jnp.zeros((LANES - third.shape[0], third.shape[1]), third.dtype)])


def third_of(table, d):
    return table[:, d * LANES : (d + 1) * LANES]


def own_kernel(shape, index, block, features, own, copy):
    nrows, width, slots, across = shape
    copy[...] = block[...]
    place = positions(block[...], nrows, across, index[0], index[1])
    own[...] = one_hot(place, 0, 3 * LANES, width, slots)


def middle_kernel(shape, index, column, own, twice):
    nrows, width, slots, across = shape
    others = jnp.concatenate([column[:nrows, :], column[2 * nrows :, :]], axis=0)
    place = positions(others, nrows, across, index[0], index[1])
    hot = one_hot(place, 0, 3 * LANES, width, slots)
    mine = own[...]
    centre = padded(jnp.concatenate([hot[:nrows], mine, hot[nrows:]], axis=0))
    known = jnp.dot(third_of(mine, 1), centre, preferred_element_type=F32)
    extra = [
        lax.dot_general(
            third_of(mine, d), third_of(centre, d), (((1,), (1,)), ((), ())), preferred_element_type=F32
        )
        for d in (0, 2)
    ]
    parts = [third_of(known, 0), third_of(known, 1) + extra[0] + extra[1], third_of(known, 2)]
    twice[...] = jnp.concatenate(parts, axis=1)


def products(weights, values):
    result, rest = None, values
    for _ in range(3):
        part = rest.astype(BF16)
        rest = rest - part.astype(F32)
        value = jnp.dot(weights, part, preferred_element_type=F32)
        result = value if result is None else result + value
    return result


def expand(result, nrows, features, shifted, old):
    turned = result.T[: features.shape[1]]
    images = [
        jnp.sum(features[b] * turned[:, nrows + b : nrows + b + 1], axis=0, keepdims=True)
        for b in range(nrows)
    ]
    return shifted * old + jnp.concatenate(images, axis=0)


def advance(step, weights, around, features, diagonal, before, moments, new, sums, block):
    nrows, width, _ = features.shape
    result = products(weights, around)
    sums[...] = result[:nrows]
    old, shifted = before[...], diagonal[...] - SHIFT
    value = expand(result, nrows, features, shifted, old)
    new[...] = value
    columns = jnp.zeros((width, LANES), F32)
    for b in range(nrows):
        columns = project(features[b], new[b : b + 1, :], columns, b)
    block[...] = to_rows(columns, nrows)
    moments = put(moments, MOMENT_LANE + 2 * step + 1, total(old * value))
    moments = put(moments, MOMENT_LANE + 2 * step + 2, total(value * value))
    if step + 2 == ITERS:
        moments = put(moments, MOMENT_LANE + 2 * step + 3, total(value * value * shifted))
    return moments


def second_kernel(
    shape, index, left, column, right, own, known, features, diagonal, before, moments,
    new, block, sums, moments_out, weights_out, tables,
):
    nrows, width, slots, across = shape
    mine = own[...]
    thirds = [third_of(known, d) for d in range(3)]
    for d, side in ((0, left), (2, right)):
        place = positions(side[...], nrows, across, index[0], index[1])
        hot = padded(one_hot(place, d * LANES, LANES, width, slots))
        thirds[d] = thirds[d] + jnp.dot(third_of(mine, d), hot, preferred_element_type=F32)
    twice = jnp.concatenate(thirds, axis=1).astype(BF16)
    pad = jnp.zeros((LANES - 2 * nrows, 3 * LANES), BF16)
    weights = jnp.concatenate([mine, twice, pad], axis=0)
    weights_out[...] = weights
    low, middle_ids, high = [side[nrows : 2 * nrows, :] for side in (left, column, right)]
    lanes = lane_iota(nrows)
    half, quarter = LANES // 2, LANES // 4
    sides = jnp.where(lanes < half, 0.0, jnp.where(lanes < half + quarter, low, pltpu.roll(high, quarter, 1)))
    tables[...] = jnp.where(lanes < half, pltpu.roll(middle_ids, half, 1), sides)
    around = jnp.concatenate([padded(side[...]) for side in (left, column, right)], axis=0)
    moments_out[...] = advance(
        0, weights, around, features, diagonal, before, moments[...], new, sums, block
    )
    block[...] = block[...] + sides


def third_kernel(
    left, column, right, weights, features, diagonal, before, moments, far,
    new, block, sums, moments_out, tables,
):
    nrows = before.shape[0]
    low, high = left[nrows : 2 * nrows, :], right[nrows : 2 * nrows, :]
    lanes = lane_iota(nrows)
    tables[...] = jnp.where(lanes < LANES * 3 // 4, low, high)
    around = jnp.concatenate([padded(side[...]) for side in (left, column, right)], axis=0)
    moments_out[...] = advance(
        1, weights[...], around, features, diagonal, before, moments[...], new, sums, block
    )


def slab_hot_kernel(shape, index, near, two, far, block, out, ids):
    nrows, width, slots, across = shape
    before, after = LANES // 2, LANES * 3 // 4
    places = ((far, 0), (far, after), (two, before), (near, before), (near, 0), (near, after), (two, after), (far, before))
    for j, (source, lane) in enumerate(places):
        ids[j] = pltpu.roll(source[...], (width - lane) % LANES, 1) if lane != width else source[...]
    span = 3 * nrows
    for a in range(across):
        table = ids[(a - index[1] + across // 2) & (across - 1)].astype(jnp.int32)
        owner = lax.shift_right_arithmetic(table, nrows.bit_length() - 1)
        offset_x = lax.shift_right_arithmetic(owner, across.bit_length() - 1) - index[0] + 1
        place = (owner & (across - 1)) * span + offset_x * nrows + (table & (nrows - 1))
        place = jnp.where((table >= 0) & (offset_x >= 0) & (offset_x < 3), place, -1)
        first = max(a - 1, 0) * span // LANES * LANES
        last = -(-min(a + 2, across) * span // LANES) * LANES
        rows = pl.ds(a * nrows, nrows)
        if first:
            out[rows, :first] = jnp.zeros((nrows, first), BF16)
        out[rows, first:last] = one_hot(place, first, last - first, width, slots)
        if last < out.shape[1]:
            out[rows, last:] = jnp.zeros((nrows, out.shape[1] - last), BF16)


def pack_kernel(up, block, down, first_sums, second_sums, moments, hot, out):
    nrows = block.shape[0]
    low = lane_iota(nrows) < LANES // 2
    top = lax.broadcasted_iota(jnp.int32, (nrows, LANES), 0) == 0
    parts = [
        jnp.where(low, up[...], pltpu.roll(first_sums[...], LANES // 2, 1)),
        jnp.where(low, block[...], pltpu.roll(second_sums[...], LANES // 2, 1)),
        jnp.where(low, down[...], jnp.where(top, moments[...], 0.0)),
    ]
    out[...] = jnp.broadcast_to(jnp.concatenate(parts, axis=0)[None], out.shape)


def slab_kernel(index, hot, slab, weights, features, diagonal, before, sums, out, new):
    across, span, _ = slab.shape
    result = products(hot[...], jnp.concatenate([slab[d] for d in range(across)], axis=0))
    sums[...] = result
    start = span // 3 * 2
    row = slab[0, start : start + 1, :]
    for d in range(1, across):
        row = row + slab[d, start : start + 1, :]
    square = total(jnp.where(lane_iota(result.shape[0]) < LANES // 2, result * result, 0.0))
    row = jnp.where(lane_iota(1) == MOMENT_LANE + MOMENTS - 1, row + square, row)
    out[...] = jnp.broadcast_to(row, out.shape)
    around = [padded(slab[(index[1] + d) & (across - 1)]) for d in (across - 1, 0, 1)]
    result = products(weights[...], jnp.concatenate(around, axis=0))
    new[...] = expand(result, features.shape[0], features, diagonal[...] - SHIFT, before[...])


def vertex_kernel(nrows, index, slab, sums, bricks, vertex_features, out):
    across, _, _ = slab.shape
    width = vertex_features.shape[0]
    local = bricks[...] - index[0] * across * nrows
    hot = lax.broadcasted_iota(jnp.int32, (across * nrows, local.shape[1]), 0) == local
    hot = jnp.where(hot, 1.0, 0.0).astype(BF16)
    table = [
        jnp.concatenate([slab[d, k * nrows : (k + 1) * nrows, :] for d in range(across)], axis=0).T[width:]
        for k in range(2)
    ]
    rest = jnp.concatenate(table + [sums[...].T[:width]], axis=0)
    picked = None
    for _ in range(3):
        part = rest.astype(BF16)
        rest = rest - part.astype(F32)
        value = jnp.dot(part, hot, preferred_element_type=F32)
        picked = value if picked is None else picked + value
    for k in range(ITERS):
        product = vertex_features[...] * picked[k * width : (k + 1) * width, :]
        out[k : k + 1, :] = jnp.sum(product, axis=0, keepdims=True)


def cg_weights(mu):
    def dot(left, right):
        return sum(left[i] * right[j] * mu[i + j] for i in range(len(left)) for j in range(len(right)))

    def apply(poly):
        out = [SHIFT * p for p in poly] + [0.0]
        for i, p in enumerate(poly):
            out[i + 1] = out[i + 1] + p
        return out

    def axpy(left, scale, right):
        size = max(len(left), len(right))
        left = left + [0.0] * (size - len(left))
        return [l + scale * right[i] if i < len(right) else l for i, l in enumerate(left)]

    field, residual, direction, norm_now = [], [1.0], [1.0], mu[0]
    for step in range(ITERS):
        image = apply(direction)
        alpha = norm_now / dot(direction, image)
        field = axpy(field, alpha, direction)
        residual = axpy(residual, -alpha, image)
        if step + 1 < ITERS:
            norm_next = dot(residual, residual)
            direction = axpy(residual, norm_next / norm_now, direction)
            norm_now = norm_next
    return field, residual


def last_kernel(moments, v0, v1, v2, v3, vertices, field_out, residual_out, vertices_out):
    sums = jnp.sum(moments[...], axis=0, keepdims=True)
    field, residual = cg_weights([sums[:, MOMENT_LANE + i : MOMENT_LANE + i + 1] for i in range(MOMENTS)])
    powers = [v0[...], v1[...], v2[...], v3[...]]
    field_out[...] = sum(w * v for w, v in zip(field, powers))
    residual_out[...] = sum(w * v for w, v in zip(residual, powers))
    vertices_out[...] = sum(w * vertices[i : i + 1, :] for i, w in enumerate(field))


def neighbourhood(block, copy=None):
    up, down = lax.ppermute(block, "gx", ring("gx", 1)), lax.ppermute(block, "gx", ring("gx", -1))
    column = jnp.concatenate([up, block if copy is None else copy, down])
    return (
        lax.ppermute(column, "gy", ring("gy", 1)),
        column,
        lax.ppermute(column, "gy", ring("gy", -1)),
    )


def per_device(right_side, diagonal, features, neighbours, vertex_features, vertex_bricks):
    nrows, width, voxels = features.shape
    slots = neighbours.shape[1]
    across, along = lax.axis_size("gy"), lax.axis_size("gx")
    index = jnp.stack([lax.axis_index("gx"), lax.axis_index("gy")]).astype(jnp.int32)
    smem, hbm = pl.BlockSpec(memory_space=pltpu.SMEM), pl.BlockSpec(memory_space=pltpu.HBM)
    shape = (nrows, width, slots, across)
    power = f32(nrows, voxels)
    block_shape, row = f32(nrows, LANES), f32(1, LANES)

    block, moments = call(
        first_kernel, [block_shape, row], features, right_side, neighbours,
        specs=[hbm] * 3, limit=FIRST_LIMIT,
        scratch=[
            pltpu.VMEM(right_side.shape, F32),
            pltpu.VMEM(neighbours.shape, jnp.int32),
            pltpu.VMEM(features.shape, F32),
            pltpu.SemaphoreType.DMA((CHUNKS + 2,)),
        ],
    )
    own, copy = call(
        functools.partial(own_kernel, shape),
        [jax.ShapeDtypeStruct((nrows, 3 * LANES), BF16), block_shape],
        index, block, features, specs=[smem, VMEM, VMEM],
    )
    left, column, right = neighbourhood(block, copy)
    known = call(
        functools.partial(middle_kernel, shape), f32(nrows, 3 * LANES),
        index, column, own, specs=[smem, VMEM, VMEM],
    )
    v1, block, first_sums, moments, weights, near = call(
        functools.partial(second_kernel, shape),
        [power, block_shape, block_shape, row, jax.ShapeDtypeStruct((LANES, 3 * LANES), BF16), block_shape],
        index, left, column, right, own, known, features, diagonal, right_side, moments,
        specs=[smem] + [VMEM] * 9,
    )
    left, column, right = neighbourhood(block)
    far = lax.ppermute(near, "gy", ring("gy", across // 2))
    v2, block, second_sums, moments, two = call(
        third_kernel, [power, block_shape, block_shape, row, block_shape],
        left, column, right, weights, features, diagonal, v1, moments, far,
    )
    up, down = lax.ppermute(block, "gx", ring("gx", 1)), lax.ppermute(block, "gx", ring("gx", -1))
    hot = call(
        functools.partial(slab_hot_kernel, shape),
        jax.ShapeDtypeStruct((across * nrows, across * 3 * nrows), BF16),
        index, near, two, far, block, specs=[smem] + [VMEM] * 4,
        scratch=[pltpu.VMEM((across, nrows, LANES), F32)],
    )
    packed = call(
        pack_kernel, f32(across, 3 * nrows, LANES),
        up, block, down, first_sums, second_sums, moments, hot,
    )
    slab = lax.all_to_all(packed, "gy", 0, 0, tiled=True)
    sums, moments, v3 = call(
        slab_kernel, [f32(across * nrows, LANES), f32(along, LANES), power],
        index, hot, slab, weights, features, diagonal, v2, specs=[smem] + [VMEM] * 6,
    )
    moments = lax.all_to_all(moments, "gx", 0, 0, tiled=True)
    vertices = call(
        functools.partial(vertex_kernel, nrows), f32(8, vertex_bricks.shape[0]),
        index, slab, sums, vertex_bricks.reshape(1, -1), vertex_features, specs=[smem] + [VMEM] * 4,
    )
    field, residual, values = call(
        last_kernel, [power, power, f32(1, vertex_bricks.shape[0])],
        moments, right_side, v1, v2, v3, vertices,
    )
    return field, residual, values.reshape(-1)


def solution(mesh):
    placed = (
        P(("gx", "gy"), None),
        P(("gx", "gy"), None),
        P(("gx", "gy"), None, None),
        P(("gx", "gy"), None),
        P(None, ("gx", "gy")),
        P(("gx", "gy")),
    )
    return jax.shard_map(
        per_device,
        mesh=mesh,
        in_specs=placed,
        out_specs=(P(("gx", "gy"), None), P(("gx", "gy"), None), P(("gx", "gy"))),
        check_vma=False,
    )
```

```python
import functools

import jax
import jax.numpy as jnp
from jax import lax
from jax.experimental import pallas as pl
from jax.experimental.pallas import tpu as pltpu
from jax.sharding import PartitionSpec as P

ITERS = 3
SHIFT = 1.25
LANES = 128
MOMENTS = 2 * ITERS
CHUNKS = 16
MOMENT_LANE = 96
FIRST_LIMIT = 60
VMEM = pl.BlockSpec(memory_space=pltpu.VMEM)
F32, BF16 = jnp.float32, jnp.bfloat16


def call(kernel, out_shape, *args, specs=None, scratch=(), limit=24):
    many = isinstance(out_shape, (list, tuple))
    return pl.pallas_call(
        kernel,
        out_shape=out_shape,
        in_specs=specs or [VMEM] * len(args),
        out_specs=[VMEM] * len(out_shape) if many else VMEM,
        scratch_shapes=scratch,
        compiler_params=pltpu.CompilerParams(vmem_limit_bytes=limit * 1024 * 1024),
    )(*args)


def f32(*shape):
    return jax.ShapeDtypeStruct(shape, F32)


def swaps(axis, first):
    count = lax.axis_size(axis)
    pairs = [(i, (i + 1) % count) for i in range(first, count, 2)]
    return pairs + [(b, a) for a, b in pairs]


def lane_iota(rows, lanes=LANES):
    return lax.broadcasted_iota(jnp.int32, (rows, lanes), 1)


def total(values):
    folded = values[:, :LANES]
    for start in range(LANES, values.shape[1], LANES):
        folded = folded + values[:, start : start + LANES]
    return jnp.sum(jnp.sum(folded, axis=0, keepdims=True), axis=1, keepdims=True)


def put(row, lane, value):
    return jnp.where(lane_iota(1) == lane, value, row)


def project(feature, field, columns, brick):
    product = feature * field
    folded = product[:, :LANES]
    for start in range(LANES, product.shape[1], LANES):
        folded = folded + product[:, start : start + LANES]
    column = jnp.sum(folded, axis=1, keepdims=True)
    return jnp.where(lane_iota(columns.shape[0]) == brick, column, columns)


def to_rows(columns, nrows):
    square = jnp.concatenate([columns, jnp.zeros((LANES - columns.shape[0], LANES), F32)], axis=0)
    return square.T[:nrows]


def first_kernel(features, field, neighbours, block, moments, values, ids, buffer, sems):
    nrows, width, _ = features.shape
    each = nrows // CHUNKS
    copies = [
        pltpu.make_async_copy(
            features.at[pl.ds(i * each, each)], buffer.at[pl.ds(i * each, each)], sems.at[i]
        )
        for i in range(CHUNKS)
    ]
    small = [
        pltpu.make_async_copy(field, values, sems.at[CHUNKS]),
        pltpu.make_async_copy(neighbours, ids, sems.at[CHUNKS + 1]),
    ]
    for copy in small + copies:
        copy.start()
    for copy in small:
        copy.wait()
    value = values[...]
    moments[...] = put(jnp.zeros((1, LANES), F32), MOMENT_LANE, total(value * value))
    columns = jnp.zeros((width, LANES), F32)
    for i, copy in enumerate(copies):
        copy.wait()
        for b in range(i * each, (i + 1) * each):
            columns = project(buffer[b], values[b : b + 1, :], columns, b)
    block[...] = to_rows(columns, nrows)
    block[:, width : width + neighbours.shape[1]] = ids[...].astype(F32)


def positions(block, nrows, across, row_index, col_index):
    ids = block.astype(jnp.int32)
    owner = lax.shift_right_arithmetic(ids, nrows.bit_length() - 1)
    offset_x = lax.shift_right_arithmetic(owner, across.bit_length() - 1) - row_index + 1
    offset_y = (owner & (across - 1)) - col_index + 1
    inside = (ids >= 0) & (offset_x >= 0) & (offset_x < 3) & (offset_y >= 0) & (offset_y < 3)
    slot_x = jnp.where((row_index & 1) == 0, 2 - offset_x, offset_x)
    slot_y = jnp.where((col_index & 1) == 0, 2 - offset_y, offset_y)
    return jnp.where(inside, slot_y * LANES + slot_x * nrows + (ids & (nrows - 1)), -1)


def one_hot(position, first, lanes, width, slots):
    targets = lane_iota(position.shape[0], lanes) + first
    out = jnp.zeros((position.shape[0], lanes), F32)
    for slot in range(width, width + slots):
        out = jnp.where(position[:, slot : slot + 1] == targets, 1.0, out)
    return out.astype(BF16)


def padded(third):
    return jnp.concatenate([third, jnp.zeros((LANES - third.shape[0], third.shape[1]), third.dtype)])


def third_of(table, d):
    return table[:, d * LANES : (d + 1) * LANES]


def own_kernel(shape, index, block, features, own, copy):
    nrows, width, slots, across = shape
    copy[...] = block[...]
    place = positions(block[...], nrows, across, index[0], index[1])
    own[...] = one_hot(place, 0, 3 * LANES, width, slots)


def middle_kernel(shape, index, column, own, twice):
    nrows, width, slots, across = shape
    others = jnp.concatenate([column[:nrows, :], column[2 * nrows :, :]], axis=0)
    place = positions(others, nrows, across, index[0], index[1])
    hot = one_hot(place, 0, 3 * LANES, width, slots)
    mine = own[...]
    centre = padded(jnp.concatenate([hot[:nrows], mine, hot[nrows:]], axis=0))
    known = jnp.dot(third_of(mine, 1), centre, preferred_element_type=F32)
    extra = [
        lax.dot_general(
            third_of(mine, d), third_of(centre, d), (((1,), (1,)), ((), ())), preferred_element_type=F32
        )
        for d in (0, 2)
    ]
    parts = [third_of(known, 0), third_of(known, 1) + extra[0] + extra[1], third_of(known, 2)]
    twice[...] = jnp.concatenate(parts, axis=1)


def advance(step, nrows, width, weights, around, features, diagonal, before, sums, moments, outs):
    last = step + 1 == ITERS
    parts = []
    rest = around
    for _ in range(3):
        part = rest.astype(BF16)
        rest = rest - part.astype(F32)
        parts.append(part)
    result = jnp.dot(weights, parts[0], preferred_element_type=F32)
    for part in parts[1:]:
        result = result + jnp.dot(weights, part, preferred_element_type=F32)
    turned = result.T[:width]
    lanes = lane_iota(width)
    shift = step * nrows
    moved = pltpu.roll(turned, shift, 1) if shift else turned
    sums = jnp.where((lanes >= shift) & (lanes < shift + nrows), moved, sums)
    old = before[...]
    images = [
        jnp.sum(features[b] * turned[:, nrows + b : nrows + b + 1], axis=0, keepdims=True)
        for b in range(nrows)
    ]
    new = (diagonal[...] - SHIFT) * old + jnp.concatenate(images, axis=0)
    outs[0][...] = new
    columns = jnp.zeros((width, LANES), F32)
    if not last:
        for b in range(nrows):
            columns = project(features[b], outs[0][b : b + 1, :], columns, b)
    moments = put(moments, MOMENT_LANE + 2 * step + 1, total(old * new))
    if not last:
        moments = put(moments, MOMENT_LANE + 2 * step + 2, total(new * new))
    return sums, moments, columns


def second_kernel(
    shape, index, left, column, right, own, known, features, diagonal, before, moments,
    new, block, sums_out, moments_out, weights_out,
):
    nrows, width, slots, across = shape
    mine = own[...]
    thirds = [third_of(known, d) for d in range(3)]
    for d, side in ((0, left), (2, right)):
        place = positions(side[...], nrows, across, index[0], index[1])
        hot = padded(one_hot(place, d * LANES, LANES, width, slots))
        thirds[d] = thirds[d] + jnp.dot(third_of(mine, d), hot, preferred_element_type=F32)
    twice = jnp.concatenate(thirds, axis=1).astype(BF16)
    pad = jnp.zeros((LANES - 2 * nrows, 3 * LANES), BF16)
    weights = jnp.concatenate([mine, twice, pad], axis=0)
    weights_out[...] = weights
    around = jnp.concatenate([padded(side[...]) for side in (left, column, right)], axis=0)
    sums, moment, columns = advance(
        0, nrows, width, weights, around, features, diagonal, before,
        jnp.zeros((width, LANES), F32), moments[...], [new],
    )
    block[...] = to_rows(columns, nrows)
    sums_out[...] = sums
    moments_out[...] = moment


def third_kernel(
    left, column, right, weights, features, diagonal, before, sums, moments,
    new, block, sums_out, moments_out,
):
    nrows, width, _ = features.shape
    around = jnp.concatenate([padded(side[...]) for side in (left, column, right)], axis=0)
    total_sums, moment, columns = advance(
        1, nrows, width, weights[...], around, features, diagonal, before,
        sums[...], moments[...], [new],
    )
    block[...] = to_rows(columns, nrows)
    sums_out[...] = total_sums
    moments_out[...] = moment


def fourth_kernel(
    left, column, right, weights, features, diagonal, before, sums, moments,
    new, sums_out,
):
    nrows, width, _ = features.shape
    around = jnp.concatenate([padded(side[...]) for side in (left, column, right)], axis=0)
    total_sums, moment, _ = advance(
        2, nrows, width, weights[...], around, features, diagonal, before,
        sums[...], moments[...], [new],
    )
    rows = lax.broadcasted_iota(jnp.int32, total_sums.shape, 0)
    mixed = total_sums + jnp.where(rows == 0, moment, 0.0)
    sums_out[...] = jnp.broadcast_to(mixed[None], sums_out.shape)


def fold_kernel(slab, out):
    row = slab[0, 0:1, :]
    for d in range(1, slab.shape[0]):
        row = row + slab[d, 0:1, :]
    out[...] = jnp.broadcast_to(row, out.shape)


def vertex_kernel(nrows, index, slab, bricks, vertex_features, out):
    across, width, _ = slab.shape
    local = bricks[...] - index[0] * across * nrows
    hot = lax.broadcasted_iota(jnp.int32, (across * nrows, local.shape[1]), 0) == local
    hot = jnp.where(hot, 1.0, 0.0).astype(BF16)
    group = LANES // nrows
    lanes = lane_iota(width)
    table = []
    for k in range(ITERS):
        tiles = []
        for start in range(0, across, group):
            tile = jnp.zeros((width, LANES), F32)
            for d in range(group):
                shift = (d - k) * nrows % LANES
                moved = pltpu.roll(slab[start + d], shift, 1) if shift else slab[start + d]
                tile = jnp.where((lanes >= d * nrows) & (lanes < (d + 1) * nrows), moved, tile)
            tiles.append(tile)
        table.append(jnp.concatenate(tiles, axis=1))
    rest = jnp.concatenate(table, axis=0)
    picked = None
    for _ in range(3):
        part = rest.astype(BF16)
        rest = rest - part.astype(F32)
        value = jnp.dot(part, hot, preferred_element_type=F32)
        picked = value if picked is None else picked + value
    for k in range(ITERS):
        product = vertex_features[...] * picked[k * width : (k + 1) * width, :]
        out[k : k + 1, :] = jnp.sum(product, axis=0, keepdims=True)


def cg_weights(mu):
    def dot(left, right):
        return sum(left[i] * right[j] * mu[i + j] for i in range(len(left)) for j in range(len(right)))

    def apply(poly):
        out = [SHIFT * p for p in poly] + [0.0]
        for i, p in enumerate(poly):
            out[i + 1] = out[i + 1] + p
        return out

    def axpy(left, scale, right):
        size = max(len(left), len(right))
        left = left + [0.0] * (size - len(left))
        return [l + scale * right[i] if i < len(right) else l for i, l in enumerate(left)]

    field, residual, direction, norm_now = [], [1.0], [1.0], mu[0]
    for step in range(ITERS):
        image = apply(direction)
        alpha = norm_now / dot(direction, image)
        field = axpy(field, alpha, direction)
        residual = axpy(residual, -alpha, image)
        if step + 1 < ITERS:
            norm_next = dot(residual, residual)
            direction = axpy(residual, norm_next / norm_now, direction)
            norm_now = norm_next
    return field, residual


def last_kernel(moments, v0, v1, v2, v3, vertices, field_out, residual_out, vertices_out):
    sums = jnp.sum(moments[...], axis=0, keepdims=True)
    field, residual = cg_weights([sums[:, MOMENT_LANE + i : MOMENT_LANE + i + 1] for i in range(MOMENTS)])
    powers = [v0[...], v1[...], v2[...], v3[...]]
    field_out[...] = sum(w * v for w, v in zip(field, powers))
    residual_out[...] = sum(w * v for w, v in zip(residual, powers))
    vertices_out[...] = sum(w * vertices[i : i + 1, :] for i, w in enumerate(field))


def neighbourhood(block, copy=None):
    second, first = lax.ppermute(block, "gx", swaps("gx", 1)), lax.ppermute(block, "gx", swaps("gx", 0))
    column = jnp.concatenate([first, block if copy is None else copy, second])
    after, before = lax.ppermute(column, "gy", swaps("gy", 1)), lax.ppermute(column, "gy", swaps("gy", 0))
    return before, column, after


def per_device(right_side, diagonal, features, neighbours, vertex_features, vertex_bricks):
    nrows, width, voxels = features.shape
    slots = neighbours.shape[1]
    across, along = lax.axis_size("gy"), lax.axis_size("gx")
    index = jnp.stack([lax.axis_index("gx"), lax.axis_index("gy")]).astype(jnp.int32)
    smem, hbm = pl.BlockSpec(memory_space=pltpu.SMEM), pl.BlockSpec(memory_space=pltpu.HBM)
    shape = (nrows, width, slots, across)
    power = f32(nrows, voxels)
    block_shape, row, table = f32(nrows, LANES), f32(1, LANES), f32(width, LANES)

    block, moments = call(
        first_kernel, [block_shape, row], features, right_side, neighbours,
        specs=[hbm] * 3, limit=FIRST_LIMIT,
        scratch=[
            pltpu.VMEM(right_side.shape, F32),
            pltpu.VMEM(neighbours.shape, jnp.int32),
            pltpu.VMEM(features.shape, F32),
            pltpu.SemaphoreType.DMA((CHUNKS + 2,)),
        ],
    )
    own, copy = call(
        functools.partial(own_kernel, shape),
        [jax.ShapeDtypeStruct((nrows, 3 * LANES), BF16), block_shape],
        index, block, features, specs=[smem, VMEM, VMEM],
    )
    left, column, right = neighbourhood(block, copy)
    known = call(
        functools.partial(middle_kernel, shape), f32(nrows, 3 * LANES),
        index, column, own, specs=[smem, VMEM, VMEM],
    )
    v1, block, sums, moments, weights = call(
        functools.partial(second_kernel, shape),
        [power, block_shape, table, row, jax.ShapeDtypeStruct((LANES, 3 * LANES), BF16)],
        index, left, column, right, own, known, features, diagonal, right_side, moments,
        specs=[smem] + [VMEM] * 9,
    )
    left, column, right = neighbourhood(block)
    v2, block, sums, moments = call(
        third_kernel, [power, block_shape, table, row],
        left, column, right, weights, features, diagonal, v1, sums, moments,
    )
    left, column, right = neighbourhood(block)
    v3, sums = call(
        fourth_kernel, [power, f32(across, width, LANES)],
        left, column, right, weights, features, diagonal, v2, sums, moments,
    )
    slab = lax.all_to_all(sums, "gy", 0, 0, tiled=True)
    moments = lax.all_to_all(call(fold_kernel, f32(along, LANES), slab), "gx", 0, 0, tiled=True)
    vertices = call(
        functools.partial(vertex_kernel, nrows), f32(8, vertex_bricks.shape[0]),
        index, slab, vertex_bricks.reshape(1, -1), vertex_features, specs=[smem] + [VMEM] * 3,
    )
    field, residual, values = call(
        last_kernel, [power, power, f32(1, vertex_bricks.shape[0])],
        moments, right_side, v1, v2, v3, vertices,
    )
    return field, residual, values.reshape(-1)


def solution(mesh):
    placed = (
        P(("gx", "gy"), None),
        P(("gx", "gy"), None),
        P(("gx", "gy"), None, None),
        P(("gx", "gy"), None),
        P(None, ("gx", "gy")),
        P(("gx", "gy")),
    )
    return jax.shard_map(
        per_device,
        mesh=mesh,
        in_specs=placed,
        out_specs=(P(("gx", "gy"), None), P(("gx", "gy"), None), P(("gx", "gy"))),
        check_vma=False,
    )
```

```python
import functools

import jax
import jax.numpy as jnp
from jax import lax
from jax.experimental import pallas as pl
from jax.experimental.pallas import tpu as pltpu
from jax.sharding import PartitionSpec as P

ITERS = 3
SHIFT = 1.25
LANES = 128
MOMENTS = 2 * ITERS
CHUNKS = 16
MOMENT_LANE = 96
FIRST_LIMIT = 60
VMEM = pl.BlockSpec(memory_space=pltpu.VMEM)
F32, BF16 = jnp.float32, jnp.bfloat16


def call(kernel, out_shape, *args, specs=None, scratch=(), limit=24):
    many = isinstance(out_shape, (list, tuple))
    return pl.pallas_call(
        kernel,
        out_shape=out_shape,
        in_specs=specs or [VMEM] * len(args),
        out_specs=[VMEM] * len(out_shape) if many else VMEM,
        scratch_shapes=scratch,
        compiler_params=pltpu.CompilerParams(vmem_limit_bytes=limit * 1024 * 1024),
    )(*args)


def f32(*shape):
    return jax.ShapeDtypeStruct(shape, F32)


def swaps(axis, first):
    count = lax.axis_size(axis)
    pairs = [(i, (i + 1) % count) for i in range(first, count, 2)]
    return pairs + [(b, a) for a, b in pairs]


def lane_iota(rows, lanes=LANES):
    return lax.broadcasted_iota(jnp.int32, (rows, lanes), 1)


def total(values):
    folded = values[:, :LANES]
    for start in range(LANES, values.shape[1], LANES):
        folded = folded + values[:, start : start + LANES]
    return jnp.sum(jnp.sum(folded, axis=0, keepdims=True), axis=1, keepdims=True)


def put(row, lane, value):
    return jnp.where(lane_iota(1) == lane, value, row)


def project(feature, field, columns, brick):
    product = feature * field
    folded = product[:, :LANES]
    for start in range(LANES, product.shape[1], LANES):
        folded = folded + product[:, start : start + LANES]
    column = jnp.sum(folded, axis=1, keepdims=True)
    return jnp.where(lane_iota(columns.shape[0]) == brick, column, columns)


def to_rows(columns, nrows):
    square = jnp.concatenate([columns, jnp.zeros((LANES - columns.shape[0], LANES), F32)], axis=0)
    return square.T[:nrows]


def first_kernel(features, field, neighbours, block, moments, values, ids, buffer, sems):
    nrows, width, _ = features.shape
    each = nrows // CHUNKS
    copies = [
        pltpu.make_async_copy(
            features.at[pl.ds(i * each, each)], buffer.at[pl.ds(i * each, each)], sems.at[i]
        )
        for i in range(CHUNKS)
    ]
    small = [
        pltpu.make_async_copy(field, values, sems.at[CHUNKS]),
        pltpu.make_async_copy(neighbours, ids, sems.at[CHUNKS + 1]),
    ]
    for copy in small + copies:
        copy.start()
    for copy in small:
        copy.wait()
    value = values[...]
    moments[...] = put(jnp.zeros((1, LANES), F32), MOMENT_LANE, total(value * value))
    columns = jnp.zeros((width, LANES), F32)
    for i, copy in enumerate(copies):
        copy.wait()
        for b in range(i * each, (i + 1) * each):
            columns = project(buffer[b], values[b : b + 1, :], columns, b)
    block[...] = to_rows(columns, nrows)
    block[:, width : width + neighbours.shape[1]] = ids[...].astype(F32)


def positions(block, nrows, across, row_index, col_index):
    ids = block.astype(jnp.int32)
    owner = lax.shift_right_arithmetic(ids, nrows.bit_length() - 1)
    offset_x = lax.shift_right_arithmetic(owner, across.bit_length() - 1) - row_index + 1
    offset_y = (owner & (across - 1)) - col_index + 1
    inside = (ids >= 0) & (offset_x >= 0) & (offset_x < 3) & (offset_y >= 0) & (offset_y < 3)
    slot_x = jnp.where((row_index & 1) == 1, 2 - offset_x, offset_x)
    slot_y = jnp.where((col_index & 1) == 0, 2 - offset_y, offset_y)
    return jnp.where(inside, slot_y * LANES + slot_x * nrows + (ids & (nrows - 1)), -1)


def one_hot(position, first, lanes, width, slots):
    targets = lane_iota(position.shape[0], lanes) + first
    out = jnp.zeros((position.shape[0], lanes), F32)
    for slot in range(width, width + slots):
        out = jnp.where(position[:, slot : slot + 1] == targets, 1.0, out)
    return out.astype(BF16)


def padded(third):
    return jnp.concatenate([third, jnp.zeros((LANES - third.shape[0], third.shape[1]), third.dtype)])


def third_of(table, d):
    return table[:, d * LANES : (d + 1) * LANES]


def own_kernel(shape, index, block, own, copy):
    nrows, width, slots, across = shape
    copy[...] = block[...]
    place = positions(block[...], nrows, across, index[0], index[1])
    own[...] = one_hot(place, 0, 3 * LANES, width, slots)


def middle_kernel(shape, index, column, own, features, twice):
    nrows, width, slots, across = shape
    others = jnp.concatenate([column[2 * nrows :, :], column[:nrows, :]], axis=0)
    place = positions(others, nrows, across, index[0], index[1])
    hot = one_hot(place, 0, 3 * LANES, width, slots)
    mine = own[...]
    centre = padded(jnp.concatenate([hot[:nrows], mine, hot[nrows:]], axis=0))
    known = jnp.dot(third_of(mine, 1), centre, preferred_element_type=F32)
    extra = [
        lax.dot_general(
            third_of(mine, d), third_of(centre, d), (((1,), (1,)), ((), ())), preferred_element_type=F32
        )
        for d in (0, 2)
    ]
    parts = [third_of(known, 0), third_of(known, 1) + extra[0] + extra[1], third_of(known, 2)]
    twice[...] = jnp.concatenate(parts, axis=1)


def advance(step, nrows, width, weights, around, features, diagonal, before, sums, moments, outs):
    last = step + 1 == ITERS
    parts = []
    rest = around
    for _ in range(3):
        part = rest.astype(BF16)
        rest = rest - part.astype(F32)
        parts.append(part)
    result = jnp.dot(weights, parts[0], preferred_element_type=F32)
    for part in parts[1:]:
        result = result + jnp.dot(weights, part, preferred_element_type=F32)
    turned = result.T[:width]
    lanes = lane_iota(width)
    shift = step * nrows
    moved = pltpu.roll(turned, shift, 1) if shift else turned
    sums = jnp.where((lanes >= shift) & (lanes < shift + nrows), moved, sums)
    old = before[...]
    images = [
        jnp.sum(features[b] * turned[:, nrows + b : nrows + b + 1], axis=0, keepdims=True)
        for b in range(nrows)
    ]
    new = (diagonal[...] - SHIFT) * old + jnp.concatenate(images, axis=0)
    outs[0][...] = new
    columns = jnp.zeros((width, LANES), F32)
    if not last:
        for b in range(nrows):
            columns = project(features[b], outs[0][b : b + 1, :], columns, b)
    moments = put(moments, MOMENT_LANE + 2 * step + 1, total(old * new))
    if not last:
        moments = put(moments, MOMENT_LANE + 2 * step + 2, total(new * new))
    return sums, moments, columns


def second_kernel(
    shape, index, left, column, right, own, known, features, diagonal, before, moments,
    new, block, sums_out, moments_out, weights_out,
):
    nrows, width, slots, across = shape
    mine = own[...]
    left, column, right = (turned_slots(side) for side in (left, column, right))
    thirds = [third_of(known, d) for d in range(3)]
    for d, side in ((0, left), (2, right)):
        place = positions(side, nrows, across, index[0], index[1])
        hot = padded(one_hot(place, d * LANES, LANES, width, slots))
        thirds[d] = thirds[d] + jnp.dot(third_of(mine, d), hot, preferred_element_type=F32)
    twice = jnp.concatenate(thirds, axis=1).astype(BF16)
    pad = jnp.zeros((LANES - 2 * nrows, 3 * LANES), BF16)
    weights = jnp.concatenate([mine, twice, pad], axis=0)
    weights_out[...] = weights
    around = jnp.concatenate([padded(side) for side in (left, column, right)], axis=0)
    sums, moment, columns = advance(
        0, nrows, width, weights, around, features, diagonal, before,
        jnp.zeros((width, LANES), F32), moments[...], [new],
    )
    block[...] = to_rows(columns, nrows)
    sums_out[...] = sums
    moments_out[...] = moment


def third_kernel(
    left, column, right, weights, features, diagonal, before, sums, moments,
    new, block, sums_out, moments_out,
):
    nrows, width, _ = features.shape
    around = jnp.concatenate([padded(side[...]) for side in (left, column, right)], axis=0)
    total_sums, moment, columns = advance(
        1, nrows, width, weights[...], around, features, diagonal, before,
        sums[...], moments[...], [new],
    )
    block[...] = to_rows(columns, nrows)
    sums_out[...] = total_sums
    moments_out[...] = moment


def fourth_kernel(
    left, column, right, weights, features, diagonal, before, sums, moments,
    new, sums_out,
):
    nrows, width, _ = features.shape
    around = jnp.concatenate([padded(side[...]) for side in (left, column, right)], axis=0)
    total_sums, moment, _ = advance(
        2, nrows, width, weights[...], around, features, diagonal, before,
        sums[...], moments[...], [new],
    )
    rows = lax.broadcasted_iota(jnp.int32, total_sums.shape, 0)
    mixed = total_sums + jnp.where(rows == 0, moment, 0.0)
    sums_out[...] = jnp.broadcast_to(mixed[None], sums_out.shape)


def fold_kernel(slab, out):
    row = slab[0, 0:1, :]
    for d in range(1, slab.shape[0]):
        row = row + slab[d, 0:1, :]
    out[...] = jnp.broadcast_to(row, out.shape)


def vertex_kernel(nrows, index, slab, bricks, vertex_features, out):
    across, width, _ = slab.shape
    local = bricks[...] - index[0] * across * nrows
    hot = lax.broadcasted_iota(jnp.int32, (across * nrows, local.shape[1]), 0) == local
    hot = jnp.where(hot, 1.0, 0.0).astype(BF16)
    group = LANES // nrows
    lanes = lane_iota(width)
    table = []
    for k in range(ITERS):
        tiles = []
        for start in range(0, across, group):
            tile = jnp.zeros((width, LANES), F32)
            for d in range(group):
                shift = (d - k) * nrows % LANES
                moved = pltpu.roll(slab[start + d], shift, 1) if shift else slab[start + d]
                tile = jnp.where((lanes >= d * nrows) & (lanes < (d + 1) * nrows), moved, tile)
            tiles.append(tile)
        table.append(jnp.concatenate(tiles, axis=1))
    rest = jnp.concatenate(table, axis=0)
    picked = None
    for _ in range(3):
        part = rest.astype(BF16)
        rest = rest - part.astype(F32)
        value = jnp.dot(part, hot, preferred_element_type=F32)
        picked = value if picked is None else picked + value
    for k in range(ITERS):
        product = vertex_features[...] * picked[k * width : (k + 1) * width, :]
        out[k : k + 1, :] = jnp.sum(product, axis=0, keepdims=True)


def cg_weights(mu):
    def dot(left, right):
        return sum(left[i] * right[j] * mu[i + j] for i in range(len(left)) for j in range(len(right)))

    def apply(poly):
        out = [SHIFT * p for p in poly] + [0.0]
        for i, p in enumerate(poly):
            out[i + 1] = out[i + 1] + p
        return out

    def axpy(left, scale, right):
        size = max(len(left), len(right))
        left = left + [0.0] * (size - len(left))
        return [l + scale * right[i] if i < len(right) else l for i, l in enumerate(left)]

    field, residual, direction, norm_now = [], [1.0], [1.0], mu[0]
    for step in range(ITERS):
        image = apply(direction)
        alpha = norm_now / dot(direction, image)
        field = axpy(field, alpha, direction)
        residual = axpy(residual, -alpha, image)
        if step + 1 < ITERS:
            norm_next = dot(residual, residual)
            direction = axpy(residual, norm_next / norm_now, direction)
            norm_now = norm_next
    return field, residual


def last_kernel(moments, v0, v1, v2, v3, vertices, field_out, residual_out, vertices_out):
    sums = jnp.sum(moments[...], axis=0, keepdims=True)
    field, residual = cg_weights([sums[:, MOMENT_LANE + i : MOMENT_LANE + i + 1] for i in range(MOMENTS)])
    powers = [v0[...], v1[...], v2[...], v3[...]]
    field_out[...] = sum(w * v for w, v in zip(field, powers))
    residual_out[...] = sum(w * v for w, v in zip(residual, powers))
    vertices_out[...] = sum(w * vertices[i : i + 1, :] for i, w in enumerate(field))


def turned_slots(side):
    nrows = side.shape[0] // 3
    return jnp.concatenate([side[2 * nrows :, :], side[nrows : 2 * nrows, :], side[:nrows, :]], axis=0)


def neighbourhood(block, copy=None):
    second, first = lax.ppermute(block, "gx", swaps("gx", 1)), lax.ppermute(block, "gx", swaps("gx", 0))
    column = jnp.concatenate([second, block, first] if copy is None else [first, copy, second])
    after, before = lax.ppermute(column, "gy", swaps("gy", 1)), lax.ppermute(column, "gy", swaps("gy", 0))
    return before, column, after


def per_device(right_side, diagonal, features, neighbours, vertex_features, vertex_bricks):
    nrows, width, voxels = features.shape
    slots = neighbours.shape[1]
    across, along = lax.axis_size("gy"), lax.axis_size("gx")
    index = jnp.stack([lax.axis_index("gx"), lax.axis_index("gy")]).astype(jnp.int32)
    smem, hbm = pl.BlockSpec(memory_space=pltpu.SMEM), pl.BlockSpec(memory_space=pltpu.HBM)
    shape = (nrows, width, slots, across)
    power = f32(nrows, voxels)
    block_shape, row, table = f32(nrows, LANES), f32(1, LANES), f32(width, LANES)

    block, moments = call(
        first_kernel, [block_shape, row], features, right_side, neighbours,
        specs=[hbm] * 3, limit=FIRST_LIMIT,
        scratch=[
            pltpu.VMEM(right_side.shape, F32),
            pltpu.VMEM(neighbours.shape, jnp.int32),
            pltpu.VMEM(features.shape, F32),
            pltpu.SemaphoreType.DMA((CHUNKS + 2,)),
        ],
    )
    own, copy = call(
        functools.partial(own_kernel, shape),
        [jax.ShapeDtypeStruct((nrows, 3 * LANES), BF16), block_shape],
        index, block, specs=[smem, VMEM],
    )
    left, column, right = neighbourhood(block, copy)
    known = call(
        functools.partial(middle_kernel, shape), f32(nrows, 3 * LANES),
        index, column, own, features, specs=[smem, VMEM, VMEM, VMEM],
    )
    v1, block, sums, moments, weights = call(
        functools.partial(second_kernel, shape),
        [power, block_shape, table, row, jax.ShapeDtypeStruct((LANES, 3 * LANES), BF16)],
        index, left, column, right, own, known, features, diagonal, right_side, moments,
        specs=[smem] + [VMEM] * 9,
    )
    left, column, right = neighbourhood(block)
    v2, block, sums, moments = call(
        third_kernel, [power, block_shape, table, row],
        left, column, right, weights, features, diagonal, v1, sums, moments,
    )
    left, column, right = neighbourhood(block)
    v3, sums = call(
        fourth_kernel, [power, f32(across, width, LANES)],
        left, column, right, weights, features, diagonal, v2, sums, moments,
    )
    slab = lax.all_to_all(sums, "gy", 0, 0, tiled=True)
    moments = lax.all_to_all(call(fold_kernel, f32(along, LANES), slab), "gx", 0, 0, tiled=True)
    vertices = call(
        functools.partial(vertex_kernel, nrows), f32(8, vertex_bricks.shape[0]),
        index, slab, vertex_bricks.reshape(1, -1), vertex_features, specs=[smem] + [VMEM] * 3,
    )
    field, residual, values = call(
        last_kernel, [power, power, f32(1, vertex_bricks.shape[0])],
        moments, right_side, v1, v2, v3, vertices,
    )
    return field, residual, values.reshape(-1)


def solution(mesh):
    placed = (
        P(("gx", "gy"), None),
        P(("gx", "gy"), None),
        P(("gx", "gy"), None, None),
        P(("gx", "gy"), None),
        P(None, ("gx", "gy")),
        P(("gx", "gy")),
    )
    return jax.shard_map(
        per_device,
        mesh=mesh,
        in_specs=placed,
        out_specs=(P(("gx", "gy"), None), P(("gx", "gy"), None), P(("gx", "gy"))),
        check_vma=False,
    )
```

```python
import functools

import jax
import jax.numpy as jnp
from jax import lax
from jax.experimental import pallas as pl
from jax.experimental.pallas import tpu as pltpu
from jax.sharding import PartitionSpec as P

ITERS = 3
SHIFT = 1.25
LANES = 128
MOMENTS = 2 * ITERS
CHUNKS = 8
MOMENT_LANE = 96
FIRST_LIMIT = 60
LIMIT = 47
VMEM = pl.BlockSpec(memory_space=pltpu.VMEM)
F32, BF16 = jnp.float32, jnp.bfloat16


def call(kernel, out_shape, *args, specs=None, scratch=(), limit=24):
    many = isinstance(out_shape, (list, tuple))
    return pl.pallas_call(
        kernel,
        out_shape=out_shape,
        in_specs=specs or [VMEM] * len(args),
        out_specs=[VMEM] * len(out_shape) if many else VMEM,
        scratch_shapes=scratch,
        compiler_params=pltpu.CompilerParams(vmem_limit_bytes=limit * 1024 * 1024),
    )(*args)


def f32(*shape):
    return jax.ShapeDtypeStruct(shape, F32)


def swaps(axis, first):
    count = lax.axis_size(axis)
    pairs = [(i, (i + 1) % count) for i in range(first, count, 2)]
    return pairs + [(b, a) for a, b in pairs]


def lane_iota(rows, lanes=LANES):
    return lax.broadcasted_iota(jnp.int32, (rows, lanes), 1)


def total(values):
    folded = values[:, :LANES]
    for start in range(LANES, values.shape[1], LANES):
        folded = folded + values[:, start : start + LANES]
    return jnp.sum(jnp.sum(folded, axis=0, keepdims=True), axis=1, keepdims=True)


def put(row, lane, value):
    return jnp.where(lane_iota(1) == lane, value, row)


def project(feature, field, columns, brick):
    product = feature * field
    folded = product[:, :LANES]
    for start in range(LANES, product.shape[1], LANES):
        folded = folded + product[:, start : start + LANES]
    column = jnp.sum(folded, axis=1, keepdims=True)
    return jnp.where(lane_iota(columns.shape[0]) == brick, column, columns)


def to_rows(columns, nrows):
    square = jnp.concatenate([columns, jnp.zeros((LANES - columns.shape[0], LANES), F32)], axis=0)
    return square.T[:nrows]


def first_kernel(features, field, neighbours, block, values, ids, buffer, sems):
    nrows, width, _ = features.shape
    each = nrows // CHUNKS
    copies = [
        pltpu.make_async_copy(
            features.at[pl.ds(i * each, each)], buffer.at[pl.ds(i * each, each)], sems.at[i]
        )
        for i in range(CHUNKS)
    ]
    small = [
        pltpu.make_async_copy(field, values, sems.at[CHUNKS]),
        pltpu.make_async_copy(neighbours, ids, sems.at[CHUNKS + 1]),
    ]
    for copy in small + copies:
        copy.start()
    for copy in small:
        copy.wait()
    columns = jnp.zeros((width, LANES), F32)
    for i, copy in enumerate(copies):
        copy.wait()
        for b in range(i * each, (i + 1) * each):
            columns = project(buffer[b], values[b : b + 1, :], columns, b)
    block[...] = to_rows(columns, nrows)
    block[:, width : width + neighbours.shape[1]] = ids[...].astype(F32)


def positions(block, nrows, across, row_index, col_index):
    ids = block.astype(jnp.int32)
    owner = lax.shift_right_arithmetic(ids, nrows.bit_length() - 1)
    offset_x = lax.shift_right_arithmetic(owner, across.bit_length() - 1) - row_index + 1
    offset_y = (owner & (across - 1)) - col_index + 1
    inside = (ids >= 0) & (offset_x >= 0) & (offset_x < 3) & (offset_y >= 0) & (offset_y < 3)
    slot_x = jnp.where((row_index & 1) == 1, 2 - offset_x, offset_x)
    slot_y = jnp.where((col_index & 1) == 0, 2 - offset_y, offset_y)
    return jnp.where(inside, slot_y * LANES + slot_x * nrows + (ids & (nrows - 1)), -1)


def one_hot(position, first, lanes, width, slots):
    targets = lane_iota(position.shape[0], lanes) + first
    out = jnp.zeros((position.shape[0], lanes), F32)
    for slot in range(width, width + slots):
        out = jnp.where(position[:, slot : slot + 1] == targets, 1.0, out)
    return out.astype(BF16)


def padded(third):
    return jnp.concatenate([third, jnp.zeros((LANES - third.shape[0], third.shape[1]), third.dtype)])


def third_of(table, d):
    return table[:, d * LANES : (d + 1) * LANES]


def own_kernel(shape, index, block, own, copy):
    nrows, width, slots, across = shape
    copy[...] = block[...]
    place = positions(block[...], nrows, across, index[0], index[1])
    own[...] = one_hot(place, 0, 3 * LANES, width, slots)


def middle_kernel(shape, index, column, own, twice):
    nrows, width, slots, across = shape
    others = jnp.concatenate([column[2 * nrows :, :], column[:nrows, :]], axis=0)
    place = positions(others, nrows, across, index[0], index[1])
    hot = one_hot(place, 0, 3 * LANES, width, slots)
    mine = own[...]
    centre = padded(jnp.concatenate([hot[:nrows], mine, hot[nrows:]], axis=0))
    known = jnp.dot(third_of(mine, 1), centre, preferred_element_type=F32)
    extra = [
        lax.dot_general(
            third_of(mine, d), third_of(centre, d), (((1,), (1,)), ((), ())), preferred_element_type=F32
        )
        for d in (0, 2)
    ]
    parts = [third_of(known, 0), third_of(known, 1) + extra[0] + extra[1], third_of(known, 2)]
    twice[...] = jnp.concatenate(parts, axis=1)


def advance(step, nrows, width, weights, around, features, diagonal, before, sums, moments, outs, copies=()):
    last = step + 1 == ITERS
    parts = []
    rest = around
    for _ in range(3):
        part = rest.astype(BF16)
        rest = rest - part.astype(F32)
        parts.append(part)
    result = jnp.dot(weights, parts[0], preferred_element_type=F32)
    for part in parts[1:]:
        result = result + jnp.dot(weights, part, preferred_element_type=F32)
    turned = result.T[:width]
    lanes = lane_iota(width)
    shift = step * nrows
    moved = pltpu.roll(turned, shift, 1) if shift else turned
    sums = jnp.where((lanes >= shift) & (lanes < shift + nrows), moved, sums)
    old = before[...]
    images = []
    for b in range(nrows):
        if copies and b % (nrows // len(copies)) == 0:
            copies[b * len(copies) // nrows].wait()
        images.append(jnp.sum(features[b] * turned[:, nrows + b : nrows + b + 1], axis=0, keepdims=True))
    new = (diagonal[...] - SHIFT) * old + jnp.concatenate(images, axis=0)
    outs[0][...] = new
    columns = jnp.zeros((width, LANES), F32)
    if not last:
        for b in range(nrows):
            columns = project(features[b], outs[0][b : b + 1, :], columns, b)
    moments = put(moments, MOMENT_LANE + 2 * step + 1, total(old * new))
    if not last:
        moments = put(moments, MOMENT_LANE + 2 * step + 2, total(new * new))
    return sums, moments, columns


def second_kernel(
    shape, index, left, column, right, own, known, far_features, diagonal, before,
    new, block, sums_out, moments_out, weights_out, features, sems,
):
    nrows, width, slots, across = shape
    each = nrows // CHUNKS
    copies = [
        pltpu.make_async_copy(
            far_features.at[pl.ds(i * each, each)], features.at[pl.ds(i * each, each)], sems.at[i]
        )
        for i in range(CHUNKS)
    ]
    for copy in copies:
        copy.start()
    mine = own[...]
    left, column, right = (turned_slots(side) for side in (left, column, right))
    thirds = [third_of(known, d) for d in range(3)]
    for d, side in ((0, left), (2, right)):
        place = positions(side, nrows, across, index[0], index[1])
        hot = padded(one_hot(place, d * LANES, LANES, width, slots))
        thirds[d] = thirds[d] + jnp.dot(third_of(mine, d), hot, preferred_element_type=F32)
    twice = jnp.concatenate(thirds, axis=1).astype(BF16)
    pad = jnp.zeros((LANES - 2 * nrows, 3 * LANES), BF16)
    weights = jnp.concatenate([mine, twice, pad], axis=0)
    weights_out[...] = weights
    around = jnp.concatenate([padded(side) for side in (left, column, right)], axis=0)
    first = put(jnp.zeros((1, LANES), F32), MOMENT_LANE, total(before[...] * before[...]))
    sums, moment, columns = advance(
        0, nrows, width, weights, around, features, diagonal, before,
        jnp.zeros((width, LANES), F32), first, [new], copies,
    )
    block[...] = to_rows(columns, nrows)
    sums_out[...] = sums
    moments_out[...] = moment


def third_kernel(
    left, column, right, weights, features, diagonal, before, sums, moments,
    new, block, sums_out, moments_out,
):
    nrows, width, _ = features.shape
    around = jnp.concatenate([padded(side[...]) for side in (left, column, right)], axis=0)
    total_sums, moment, columns = advance(
        1, nrows, width, weights[...], around, features, diagonal, before,
        sums[...], moments[...], [new],
    )
    block[...] = to_rows(columns, nrows)
    sums_out[...] = total_sums
    moments_out[...] = moment


def fourth_kernel(
    left, column, right, weights, features, diagonal, before, sums, moments,
    new, sums_out,
):
    nrows, width, _ = features.shape
    around = jnp.concatenate([padded(side[...]) for side in (left, column, right)], axis=0)
    total_sums, moment, _ = advance(
        2, nrows, width, weights[...], around, features, diagonal, before,
        sums[...], moments[...], [new],
    )
    rows = lax.broadcasted_iota(jnp.int32, total_sums.shape, 0)
    mixed = total_sums + jnp.where(rows == 0, moment, 0.0)
    sums_out[...] = jnp.broadcast_to(mixed[None], sums_out.shape)


def fold_kernel(slab, out):
    row = slab[0, 0:1, :]
    for d in range(1, slab.shape[0]):
        row = row + slab[d, 0:1, :]
    out[...] = jnp.broadcast_to(row, out.shape)


def vertex_kernel(nrows, index, slab, bricks, vertex_features, out):
    across, width, _ = slab.shape
    local = bricks[...] - index[0] * across * nrows
    hot = lax.broadcasted_iota(jnp.int32, (across * nrows, local.shape[1]), 0) == local
    hot = jnp.where(hot, 1.0, 0.0).astype(BF16)
    group = LANES // nrows
    lanes = lane_iota(width)
    table = []
    for k in range(ITERS):
        tiles = []
        for start in range(0, across, group):
            tile = jnp.zeros((width, LANES), F32)
            for d in range(group):
                shift = (d - k) * nrows % LANES
                moved = pltpu.roll(slab[start + d], shift, 1) if shift else slab[start + d]
                tile = jnp.where((lanes >= d * nrows) & (lanes < (d + 1) * nrows), moved, tile)
            tiles.append(tile)
        table.append(jnp.concatenate(tiles, axis=1))
    rest = jnp.concatenate(table, axis=0)
    picked = None
    for _ in range(3):
        part = rest.astype(BF16)
        rest = rest - part.astype(F32)
        value = jnp.dot(part, hot, preferred_element_type=F32)
        picked = value if picked is None else picked + value
    for k in range(ITERS):
        product = vertex_features[...] * picked[k * width : (k + 1) * width, :]
        out[k : k + 1, :] = jnp.sum(product, axis=0, keepdims=True)


def cg_weights(mu):
    def dot(left, right):
        return sum(left[i] * right[j] * mu[i + j] for i in range(len(left)) for j in range(len(right)))

    def apply(poly):
        out = [SHIFT * p for p in poly] + [0.0]
        for i, p in enumerate(poly):
            out[i + 1] = out[i + 1] + p
        return out

    def axpy(left, scale, right):
        size = max(len(left), len(right))
        left = left + [0.0] * (size - len(left))
        return [l + scale * right[i] if i < len(right) else l for i, l in enumerate(left)]

    field, residual, direction, norm_now = [], [1.0], [1.0], mu[0]
    for step in range(ITERS):
        image = apply(direction)
        alpha = norm_now / dot(direction, image)
        field = axpy(field, alpha, direction)
        residual = axpy(residual, -alpha, image)
        if step + 1 < ITERS:
            norm_next = dot(residual, residual)
            direction = axpy(residual, norm_next / norm_now, direction)
            norm_now = norm_next
    return field, residual


def last_kernel(moments, v0, v1, v2, v3, vertices, field_out, residual_out, vertices_out):
    sums = jnp.sum(moments[...], axis=0, keepdims=True)
    field, residual = cg_weights([sums[:, MOMENT_LANE + i : MOMENT_LANE + i + 1] for i in range(MOMENTS)])
    powers = [v0[...], v1[...], v2[...], v3[...]]
    field_out[...] = sum(w * v for w, v in zip(field, powers))
    residual_out[...] = sum(w * v for w, v in zip(residual, powers))
    vertices_out[...] = sum(w * vertices[i : i + 1, :] for i, w in enumerate(field))


def turned_slots(side):
    nrows = side.shape[0] // 3
    return jnp.concatenate([side[2 * nrows :, :], side[nrows : 2 * nrows, :], side[:nrows, :]], axis=0)


def neighbourhood(block, copy=None):
    second, first = lax.ppermute(block, "gx", swaps("gx", 1)), lax.ppermute(block, "gx", swaps("gx", 0))
    column = jnp.concatenate([second, block, first] if copy is None else [first, copy, second])
    after, before = lax.ppermute(column, "gy", swaps("gy", 1)), lax.ppermute(column, "gy", swaps("gy", 0))
    return before, column, after


def per_device(right_side, diagonal, features, neighbours, vertex_features, vertex_bricks):
    nrows, width, voxels = features.shape
    slots = neighbours.shape[1]
    across, along = lax.axis_size("gy"), lax.axis_size("gx")
    index = jnp.stack([lax.axis_index("gx"), lax.axis_index("gy")]).astype(jnp.int32)
    smem, hbm = pl.BlockSpec(memory_space=pltpu.SMEM), pl.BlockSpec(memory_space=pltpu.HBM)
    shape = (nrows, width, slots, across)
    power = f32(nrows, voxels)
    block_shape, row, table = f32(nrows, LANES), f32(1, LANES), f32(width, LANES)

    block = call(
        first_kernel, block_shape, features, right_side, neighbours,
        specs=[hbm] * 3, limit=FIRST_LIMIT,
        scratch=[
            pltpu.VMEM(right_side.shape, F32),
            pltpu.VMEM(neighbours.shape, jnp.int32),
            pltpu.VMEM(features.shape, F32),
            pltpu.SemaphoreType.DMA((CHUNKS + 2,)),
        ],
    )
    own, copy = call(
        functools.partial(own_kernel, shape),
        [jax.ShapeDtypeStruct((nrows, 3 * LANES), BF16), block_shape],
        index, block, specs=[smem, VMEM],
    )
    left, column, right = neighbourhood(block, copy)
    known = call(
        functools.partial(middle_kernel, shape), f32(nrows, 3 * LANES),
        index, column, own, specs=[smem, VMEM, VMEM],
    )
    v1, block, sums, moments, weights, features = call(
        functools.partial(second_kernel, shape),
        [
            power, block_shape, table, row, jax.ShapeDtypeStruct((LANES, 3 * LANES), BF16),
            f32(*features.shape),
        ],
        index, left, column, right, own, known, features, diagonal, right_side,
        specs=[smem] + [VMEM] * 5 + [hbm] + [VMEM] * 2, limit=LIMIT,
        scratch=[pltpu.SemaphoreType.DMA((CHUNKS,))],
    )
    left, column, right = neighbourhood(block)
    v2, block, sums, moments = call(
        third_kernel, [power, block_shape, table, row],
        left, column, right, weights, features, diagonal, v1, sums, moments,
    )
    left, column, right = neighbourhood(block)
    v3, sums = call(
        fourth_kernel, [power, f32(across, width, LANES)],
        left, column, right, weights, features, diagonal, v2, sums, moments,
    )
    slab = lax.all_to_all(sums, "gy", 0, 0, tiled=True)
    moments = lax.all_to_all(call(fold_kernel, f32(along, LANES), slab), "gx", 0, 0, tiled=True)
    vertices = call(
        functools.partial(vertex_kernel, nrows), f32(8, vertex_bricks.shape[0]),
        index, slab, vertex_bricks.reshape(1, -1), vertex_features, specs=[smem] + [VMEM] * 3,
    )
    field, residual, values = call(
        last_kernel, [power, power, f32(1, vertex_bricks.shape[0])],
        moments, right_side, v1, v2, v3, vertices,
    )
    return field, residual, values.reshape(-1)


def solution(mesh):
    placed = (
        P(("gx", "gy"), None),
        P(("gx", "gy"), None),
        P(("gx", "gy"), None, None),
        P(("gx", "gy"), None),
        P(None, ("gx", "gy")),
        P(("gx", "gy")),
    )
    return jax.shard_map(
        per_device,
        mesh=mesh,
        in_specs=placed,
        out_specs=(P(("gx", "gy"), None), P(("gx", "gy"), None), P(("gx", "gy"))),
        check_vma=False,
    )
```

```python
import functools

import jax
import jax.numpy as jnp
from jax import lax
from jax.experimental import pallas as pl
from jax.experimental.pallas import tpu as pltpu
from jax.sharding import PartitionSpec as P

ITERS = 3
SHIFT = 1.25
LANES = 128
MOMENTS = 2 * ITERS
CHUNKS = 8
MOMENT_LANE = 96
FIRST_LIMIT = 60
VMEM = pl.BlockSpec(memory_space=pltpu.VMEM)
F32, BF16 = jnp.float32, jnp.bfloat16


def call(kernel, out_shape, *args, specs=None, scratch=(), limit=24):
    many = isinstance(out_shape, (list, tuple))
    return pl.pallas_call(
        kernel,
        out_shape=out_shape,
        in_specs=specs or [VMEM] * len(args),
        out_specs=[VMEM] * len(out_shape) if many else VMEM,
        scratch_shapes=scratch,
        compiler_params=pltpu.CompilerParams(vmem_limit_bytes=limit * 1024 * 1024),
    )(*args)


def f32(*shape):
    return jax.ShapeDtypeStruct(shape, F32)


def swaps(axis, first):
    count = lax.axis_size(axis)
    pairs = [(i, (i + 1) % count) for i in range(first, count, 2)]
    return pairs + [(b, a) for a, b in pairs]


def lane_iota(rows, lanes=LANES):
    return lax.broadcasted_iota(jnp.int32, (rows, lanes), 1)


def total(values):
    folded = values[:, :LANES]
    for start in range(LANES, values.shape[1], LANES):
        folded = folded + values[:, start : start + LANES]
    return jnp.sum(jnp.sum(folded, axis=0, keepdims=True), axis=1, keepdims=True)


def put(row, lane, value):
    return jnp.where(lane_iota(1) == lane, value, row)


def project(feature, field, columns, brick):
    product = feature * field
    folded = product[:, :LANES]
    for start in range(LANES, product.shape[1], LANES):
        folded = folded + product[:, start : start + LANES]
    column = jnp.sum(folded, axis=1, keepdims=True)
    return jnp.where(lane_iota(columns.shape[0]) == brick, column, columns)


def to_rows(columns, nrows):
    square = jnp.concatenate([columns, jnp.zeros((LANES - columns.shape[0], LANES), F32)], axis=0)
    return square.T[:nrows]


def first_kernel(features, field, neighbours, block, moments, values, ids, buffer, sems):
    nrows, width, _ = features.shape
    each = nrows // CHUNKS
    copies = [
        pltpu.make_async_copy(
            features.at[pl.ds(i * each, each)], buffer.at[pl.ds(i * each, each)], sems.at[i]
        )
        for i in range(CHUNKS)
    ]
    small = [
        pltpu.make_async_copy(field, values, sems.at[CHUNKS]),
        pltpu.make_async_copy(neighbours, ids, sems.at[CHUNKS + 1]),
    ]
    for copy in small + copies:
        copy.start()
    for copy in small:
        copy.wait()
    value = values[...]
    moments[...] = put(jnp.zeros((1, LANES), F32), MOMENT_LANE, total(value * value))
    columns = jnp.zeros((width, LANES), F32)
    for i, copy in enumerate(copies):
        copy.wait()
        for b in range(i * each, (i + 1) * each):
            columns = project(buffer[b], values[b : b + 1, :], columns, b)
    block[...] = to_rows(columns, nrows)
    block[:, width : width + neighbours.shape[1]] = ids[...].astype(F32)


def positions(block, nrows, across, row_index, col_index):
    ids = block.astype(jnp.int32)
    owner = lax.shift_right_arithmetic(ids, nrows.bit_length() - 1)
    offset_x = lax.shift_right_arithmetic(owner, across.bit_length() - 1) - row_index + 1
    offset_y = (owner & (across - 1)) - col_index + 1
    inside = (ids >= 0) & (offset_x >= 0) & (offset_x < 3) & (offset_y >= 0) & (offset_y < 3)
    slot_x = jnp.where((row_index & 1) == 1, 2 - offset_x, offset_x)
    slot_y = jnp.where((col_index & 1) == 0, 2 - offset_y, offset_y)
    return jnp.where(inside, slot_y * LANES + slot_x * nrows + (ids & (nrows - 1)), -1)


def one_hot(position, first, lanes, width, slots):
    targets = lane_iota(position.shape[0], lanes) + first
    out = jnp.zeros((position.shape[0], lanes), F32)
    for slot in range(width, width + slots):
        out = jnp.where(position[:, slot : slot + 1] == targets, 1.0, out)
    return out.astype(BF16)


def padded(third):
    return jnp.concatenate([third, jnp.zeros((LANES - third.shape[0], third.shape[1]), third.dtype)])


def third_of(table, d):
    return table[:, d * LANES : (d + 1) * LANES]


def own_kernel(shape, index, block, own, copy):
    nrows, width, slots, across = shape
    copy[...] = block[...]
    place = positions(block[...], nrows, across, index[0], index[1])
    own[...] = one_hot(place, 0, 3 * LANES, width, slots)


def middle_kernel(shape, index, column, own, features, twice):
    nrows, width, slots, across = shape
    others = jnp.concatenate([column[2 * nrows :, :], column[:nrows, :]], axis=0)
    place = positions(others, nrows, across, index[0], index[1])
    hot = one_hot(place, 0, 3 * LANES, width, slots)
    mine = own[...]
    centre = padded(jnp.concatenate([hot[:nrows], mine, hot[nrows:]], axis=0))
    known = jnp.dot(third_of(mine, 1), centre, preferred_element_type=F32)
    extra = [
        lax.dot_general(
            third_of(mine, d), third_of(centre, d), (((1,), (1,)), ((), ())), preferred_element_type=F32
        )
        for d in (0, 2)
    ]
    parts = [third_of(known, 0), third_of(known, 1) + extra[0] + extra[1], third_of(known, 2)]
    twice[...] = jnp.concatenate(parts, axis=1)


def advance(step, nrows, width, weights, around, features, diagonal, before, sums, moments, outs):
    last = step + 1 == ITERS
    parts = []
    rest = around
    for _ in range(3):
        part = rest.astype(BF16)
        rest = rest - part.astype(F32)
        parts.append(part)
    result = jnp.dot(weights, parts[0], preferred_element_type=F32)
    for part in parts[1:]:
        result = result + jnp.dot(weights, part, preferred_element_type=F32)
    turned = result.T[:width]
    lanes = lane_iota(width)
    shift = step * nrows
    moved = pltpu.roll(turned, shift, 1) if shift else turned
    sums = jnp.where((lanes >= shift) & (lanes < shift + nrows), moved, sums)
    old = before[...]
    images = [
        jnp.sum(features[b] * turned[:, nrows + b : nrows + b + 1], axis=0, keepdims=True)
        for b in range(nrows)
    ]
    new = (diagonal[...] - SHIFT) * old + jnp.concatenate(images, axis=0)
    outs[0][...] = new
    columns = jnp.zeros((width, LANES), F32)
    if not last:
        for b in range(nrows):
            columns = project(features[b], outs[0][b : b + 1, :], columns, b)
    moments = put(moments, MOMENT_LANE + 2 * step + 1, total(old * new))
    if not last:
        moments = put(moments, MOMENT_LANE + 2 * step + 2, total(new * new))
    return sums, moments, columns


def second_kernel(
    shape, index, left, column, right, own, known, features, diagonal, before, moments,
    new, block, sums_out, moments_out, weights_out,
):
    nrows, width, slots, across = shape
    mine = own[...]
    left, column, right = (turned_slots(side) for side in (left, column, right))
    thirds = [third_of(known, d) for d in range(3)]
    for d, side in ((0, left), (2, right)):
        place = positions(side, nrows, across, index[0], index[1])
        hot = padded(one_hot(place, d * LANES, LANES, width, slots))
        thirds[d] = thirds[d] + jnp.dot(third_of(mine, d), hot, preferred_element_type=F32)
    twice = jnp.concatenate(thirds, axis=1).astype(BF16)
    pad = jnp.zeros((LANES - 2 * nrows, 3 * LANES), BF16)
    weights = jnp.concatenate([mine, twice, pad], axis=0)
    weights_out[...] = weights
    around = jnp.concatenate([padded(side) for side in (left, column, right)], axis=0)
    sums, moment, columns = advance(
        0, nrows, width, weights, around, features, diagonal, before,
        jnp.zeros((width, LANES), F32), moments[...], [new],
    )
    block[...] = to_rows(columns, nrows)
    sums_out[...] = sums
    moments_out[...] = moment


def third_kernel(
    left, column, right, weights, features, diagonal, before, sums, moments,
    new, block, sums_out, moments_out,
):
    nrows, width, _ = features.shape
    around = jnp.concatenate([padded(side[...]) for side in (left, column, right)], axis=0)
    total_sums, moment, columns = advance(
        1, nrows, width, weights[...], around, features, diagonal, before,
        sums[...], moments[...], [new],
    )
    block[...] = to_rows(columns, nrows)
    sums_out[...] = total_sums
    moments_out[...] = moment


def fourth_kernel(
    left, column, right, weights, features, diagonal, before, sums, moments,
    new, sums_out,
):
    nrows, width, _ = features.shape
    around = jnp.concatenate([padded(side[...]) for side in (left, column, right)], axis=0)
    total_sums, moment, _ = advance(
        2, nrows, width, weights[...], around, features, diagonal, before,
        sums[...], moments[...], [new],
    )
    rows = lax.broadcasted_iota(jnp.int32, total_sums.shape, 0)
    mixed = total_sums + jnp.where(rows == 0, moment, 0.0)
    sums_out[...] = jnp.broadcast_to(mixed[None], sums_out.shape)


def fold_kernel(slab, out):
    row = slab[0, 0:1, :]
    for d in range(1, slab.shape[0]):
        row = row + slab[d, 0:1, :]
    out[...] = jnp.broadcast_to(row, out.shape)


def vertex_kernel(nrows, index, slab, bricks, vertex_features, out):
    across, width, _ = slab.shape
    local = bricks[...] - index[0] * across * nrows
    hot = lax.broadcasted_iota(jnp.int32, (across * nrows, local.shape[1]), 0) == local
    hot = jnp.where(hot, 1.0, 0.0).astype(BF16)
    group = LANES // nrows
    lanes = lane_iota(width)
    table = []
    for k in range(ITERS):
        tiles = []
        for start in range(0, across, group):
            tile = jnp.zeros((width, LANES), F32)
            for d in range(group):
                shift = (d - k) * nrows % LANES
                moved = pltpu.roll(slab[start + d], shift, 1) if shift else slab[start + d]
                tile = jnp.where((lanes >= d * nrows) & (lanes < (d + 1) * nrows), moved, tile)
            tiles.append(tile)
        table.append(jnp.concatenate(tiles, axis=1))
    rest = jnp.concatenate(table, axis=0)
    picked = None
    for _ in range(3):
        part = rest.astype(BF16)
        rest = rest - part.astype(F32)
        value = jnp.dot(part, hot, preferred_element_type=F32)
        picked = value if picked is None else picked + value
    for k in range(ITERS):
        product = vertex_features[...] * picked[k * width : (k + 1) * width, :]
        out[k : k + 1, :] = jnp.sum(product, axis=0, keepdims=True)


def cg_weights(mu):
    def dot(left, right):
        return sum(left[i] * right[j] * mu[i + j] for i in range(len(left)) for j in range(len(right)))

    def apply(poly):
        out = [SHIFT * p for p in poly] + [0.0]
        for i, p in enumerate(poly):
            out[i + 1] = out[i + 1] + p
        return out

    def axpy(left, scale, right):
        size = max(len(left), len(right))
        left = left + [0.0] * (size - len(left))
        return [l + scale * right[i] if i < len(right) else l for i, l in enumerate(left)]

    field, residual, direction, norm_now = [], [1.0], [1.0], mu[0]
    for step in range(ITERS):
        image = apply(direction)
        alpha = norm_now / dot(direction, image)
        field = axpy(field, alpha, direction)
        residual = axpy(residual, -alpha, image)
        if step + 1 < ITERS:
            norm_next = dot(residual, residual)
            direction = axpy(residual, norm_next / norm_now, direction)
            norm_now = norm_next
    return field, residual


def last_kernel(moments, v0, v1, v2, v3, vertices, field_out, residual_out, vertices_out):
    sums = jnp.sum(moments[...], axis=0, keepdims=True)
    field, residual = cg_weights([sums[:, MOMENT_LANE + i : MOMENT_LANE + i + 1] for i in range(MOMENTS)])
    powers = [v0[...], v1[...], v2[...], v3[...]]
    field_out[...] = sum(w * v for w, v in zip(field, powers))
    residual_out[...] = sum(w * v for w, v in zip(residual, powers))
    vertices_out[...] = sum(w * vertices[i : i + 1, :] for i, w in enumerate(field))


def turned_slots(side):
    nrows = side.shape[0] // 3
    return jnp.concatenate([side[2 * nrows :, :], side[nrows : 2 * nrows, :], side[:nrows, :]], axis=0)


def neighbourhood(block, copy=None):
    second, first = lax.ppermute(block, "gx", swaps("gx", 1)), lax.ppermute(block, "gx", swaps("gx", 0))
    column = jnp.concatenate([second, block, first] if copy is None else [first, copy, second])
    after, before = lax.ppermute(column, "gy", swaps("gy", 1)), lax.ppermute(column, "gy", swaps("gy", 0))
    return before, column, after


def per_device(right_side, diagonal, features, neighbours, vertex_features, vertex_bricks):
    nrows, width, voxels = features.shape
    slots = neighbours.shape[1]
    across, along = lax.axis_size("gy"), lax.axis_size("gx")
    index = jnp.stack([lax.axis_index("gx"), lax.axis_index("gy")]).astype(jnp.int32)
    smem, hbm = pl.BlockSpec(memory_space=pltpu.SMEM), pl.BlockSpec(memory_space=pltpu.HBM)
    shape = (nrows, width, slots, across)
    power = f32(nrows, voxels)
    block_shape, row, table = f32(nrows, LANES), f32(1, LANES), f32(width, LANES)

    block, moments = call(
        first_kernel, [block_shape, row], features, right_side, neighbours,
        specs=[hbm] * 3, limit=FIRST_LIMIT,
        scratch=[
            pltpu.VMEM(right_side.shape, F32),
            pltpu.VMEM(neighbours.shape, jnp.int32),
            pltpu.VMEM(features.shape, F32),
            pltpu.SemaphoreType.DMA((CHUNKS + 2,)),
        ],
    )
    own, copy = call(
        functools.partial(own_kernel, shape),
        [jax.ShapeDtypeStruct((nrows, 3 * LANES), BF16), block_shape],
        index, block, specs=[smem, VMEM],
    )
    left, column, right = neighbourhood(block, copy)
    known = call(
        functools.partial(middle_kernel, shape), f32(nrows, 3 * LANES),
        index, column, own, features, specs=[smem, VMEM, VMEM, VMEM],
    )
    v1, block, sums, moments, weights = call(
        functools.partial(second_kernel, shape),
        [power, block_shape, table, row, jax.ShapeDtypeStruct((LANES, 3 * LANES), BF16)],
        index, left, column, right, own, known, features, diagonal, right_side, moments,
        specs=[smem] + [VMEM] * 9,
    )
    left, column, right = neighbourhood(block)
    v2, block, sums, moments = call(
        third_kernel, [power, block_shape, table, row],
        left, column, right, weights, features, diagonal, v1, sums, moments,
    )
    left, column, right = neighbourhood(block)
    v3, sums = call(
        fourth_kernel, [power, f32(across, width, LANES)],
        left, column, right, weights, features, diagonal, v2, sums, moments,
    )
    slab = lax.all_to_all(sums, "gy", 0, 0, tiled=True)
    moments = lax.all_to_all(call(fold_kernel, f32(along, LANES), slab), "gx", 0, 0, tiled=True)
    vertices = call(
        functools.partial(vertex_kernel, nrows), f32(8, vertex_bricks.shape[0]),
        index, slab, vertex_bricks.reshape(1, -1), vertex_features, specs=[smem] + [VMEM] * 3,
    )
    field, residual, values = call(
        last_kernel, [power, power, f32(1, vertex_bricks.shape[0])],
        moments, right_side, v1, v2, v3, vertices,
    )
    return field, residual, values.reshape(-1)


def solution(mesh):
    placed = (
        P(("gx", "gy"), None),
        P(("gx", "gy"), None),
        P(("gx", "gy"), None, None),
        P(("gx", "gy"), None),
        P(None, ("gx", "gy")),
        P(("gx", "gy")),
    )
    return jax.shard_map(
        per_device,
        mesh=mesh,
        in_specs=placed,
        out_specs=(P(("gx", "gy"), None), P(("gx", "gy"), None), P(("gx", "gy"))),
        check_vma=False,
    )
```
